128 devices in a mesh: seq: 16 (over z_lo, y, core), head: 8 (over z_hi, x).
Axes of the slice: x: 4, y: 4, z: 4 (z_hi: 2, z_lo: 2; z = z_hi * 2 + z_lo), core: 2. Of those that a mesh axis runs over, the one named last changes fastest.
Arguments:
- queries: bfloat16 [8192, 4096], P('seq', 'head'), may hold values from -6 to 6
- new_keys: bfloat16 [8192, 4096], P('seq', 'head'), may hold values from -6 to 6
- new_values: bfloat16 [8192, 4096], P('seq', 'head'), may hold values from -6 to 6
- pool_keys: bfloat16 [16384, 4096], P('seq', 'head'), may hold values from -6 to 6
- pool_values: bfloat16 [16384, 4096], P('seq', 'head'), may hold values from -6 to 6
- cache_len: int32 [4], replicated, may hold values from 128 to 4096, as said below
- cached_table: int32 [4, 32], replicated, may hold values from -1 to 127, as said below
- free_blocks: int32 [4, 16], replicated, may hold values from 0 to 127, as said below
- residual_in: bfloat16 [8192, 7168], P('seq', 'head'), may hold values from -26 to 26
- out_weight: bfloat16 [4096, 7168], P('head'), may hold values from -2.390625 to 2.390625
- out_bias: float32 [7168], P('head'), may hold values from -3 to 3
- ln_gain: float32 [7168], P('head'), may hold values from 0.1 to 1.9
- ln_bias: float32 [7168], P('head'), may hold values from -3 to 3
Outputs:
- hidden: bfloat16 [8192, 7168], P('seq', 'head')
- normed: bfloat16 [8192, 7168], P('seq', 'head')
- keys_out: bfloat16 [16384, 4096], P('seq', 'head')
- values_out: bfloat16 [16384, 4096], P('seq', 'head')
The draws below stay inside these ranges and needn't reach their ends.
Inputs may be any that keep to these rules, and one draw needn't show every extreme that they name: `cache_len`: a multiple of 128; exactly one prompt has 4096 cached positions. `cached_table`: entry [p, j] names the pool block that holds cached positions j * 128 to j * 128 + 127 of prompt p when j < cache_len[p] / 128, and is -1 otherwise; the named blocks are all different and lie anywhere in the pool. `free_blocks`: all different and never named by cached_table; block free_blocks[p, j] lies in the pool rows held by the same index of seq as token row p * 2048 + j * 128, that is free_blocks[p, j] * 128 // 1024 == (p * 2048 + j * 128) // 512.
All inputs are finite; a program needn't handle non-finite values.
Results may differ from the reference program's by a relative error of at most 0.022.
Values may be sent and summed in bfloat16 or wider, within the bound.
No kernel may reach another device: no remote copies, remote signals or barrier semaphores. Data moves between devices by JAX's collectives and lax.ppermute only.
A program may use at most 384 MiB of HBM per device.

```python
import jax
import jax.numpy as jnp
from jax import lax

D = 7168
HEADS = 32
HD = 128
TOK_DEV = 512
NEW_LEN = 2048
BLOCK = 128
CACHE_MAX = 4096
TOKENS = 8192
PROMPTS = 4
POOL_DEV = 1024
POOL = 16384
N_HEAD = 8


def block_plan(key):
    per_device = POOL_DEV // BLOCK
    devices_seq = POOL // POOL_DEV
    fresh_device = TOK_DEV // BLOCK
    cached_blocks = CACHE_MAX // BLOCK
    fresh_prompt = NEW_LEN // BLOCK
    keys_all = jax.random.split(jax.random.fold_in(key, 71), 4)
    local_order = jax.vmap(lambda single: jax.random.permutation(single, per_device))(jax.random.split(keys_all[0], devices_seq))
    blocks = (local_order + (jnp.arange(devices_seq) * per_device)[:, None]).astype(jnp.int32)
    free_list = blocks[:, :fresh_device].reshape(PROMPTS, fresh_prompt)
    remaining = jax.random.permutation(keys_all[1], blocks[:, fresh_device:].reshape(-1)).astype(jnp.int32)
    longest = jax.random.randint(keys_all[2], (), 0, PROMPTS)
    others = jax.random.randint(keys_all[3], (PROMPTS,), 1, cached_blocks // (PROMPTS - 1) + 1)
    counts = jnp.where(jnp.arange(PROMPTS) == longest, cached_blocks, others).astype(jnp.int32)
    offsets = jnp.cumsum(counts) - counts
    far_device = (longest * (NEW_LEN // TOK_DEV) + devices_seq // 2) % devices_seq
    chosen = blocks[far_device, fresh_device]
    spot = offsets[longest]
    found = jnp.argmax((remaining == chosen).astype(jnp.int32))
    displaced = remaining[spot]
    remaining = remaining.at[found].set(displaced).at[spot].set(chosen)
    slots = jnp.arange(cached_blocks, dtype=jnp.int32)
    where_from = jnp.clip(offsets[:, None] + slots[None, :], 0, remaining.shape[0] - 1)
    table = jnp.where(slots[None, :] < counts[:, None], remaining[where_from], -1).astype(jnp.int32)
    return ((counts * BLOCK).astype(jnp.int32), table, free_list.astype(jnp.int32))


def draw_cache_len(key, part):
    return block_plan(key)[0]


def draw_cached_table(key, part):
    return block_plan(key)[1]


def draw_free_blocks(key, part):
    return block_plan(key)[2]


def draw_queries(key, part):
    base = jnp.clip(jax.random.normal(jax.random.fold_in(key, 1), (TOKENS, HEADS * HD), jnp.float32), -6.0, 6.0)
    return base.astype(jnp.bfloat16)


def draw_new_keys(key, part):
    base = jnp.clip(jax.random.normal(jax.random.fold_in(key, 2), (TOKENS, HEADS * HD), jnp.float32), -6.0, 6.0)
    return base.astype(jnp.bfloat16)


def draw_residual_in(key, part):
    keys_all = jax.random.split(jax.random.fold_in(key, 5), 2)
    columns = jnp.arange(D, dtype=jnp.float32)
    column_scale = jnp.exp(jnp.log(3.0) * columns / D) * jnp.exp(jax.random.uniform(keys_all[0], (D,), jnp.float32, -0.35, 0.35))
    offset = 0.4 + 1.6 * columns / D
    values = jnp.clip(jax.random.normal(keys_all[1], (TOKENS, D), jnp.float32), -5.0, 5.0) * column_scale[None, :] + offset[None, :]
    return values.astype(jnp.bfloat16)


def level_of(rng, dims, shards, least, top_value):
    level = 1.0
    for position, parts in shards:
        heights = jax.random.uniform(jax.random.fold_in(jax.random.fold_in(rng, 6), position), (parts,), jnp.float32, least / len(shards), top_value / len(shards))
        level = level * jnp.repeat(jnp.exp(heights), dims[position] // parts).reshape((-1,) + (1,) * (len(dims) - 1 - position))
    return level


def gaussian(stream_key, extent, deviation, reach, cuts=(), held_as=jnp.bfloat16):
    gain = level_of(stream_key, extent, cuts, -0.22, 0.18) if cuts else 1.0
    array = jax.random.normal(stream_key, extent, jnp.float32) * deviation * gain
    return jnp.minimum(jnp.maximum(array, -reach), reach).astype(held_as)


def setup_inputs(seed: int = 0) -> dict:
    seeds = jax.random.split(jax.random.key(seed), 14)
    return {
        "queries": draw_queries(jax.random.fold_in(seeds[13], 71), 0),
        "new_keys": draw_new_keys(jax.random.fold_in(seeds[13], 71), 0),
        "new_values": gaussian(seeds[2], (TOKENS, HEADS * HD), 1.0, 6.0, ((0, 16), (1, 8))),
        "pool_keys": gaussian(seeds[3], (POOL, HEADS * HD), 1.0, 6.0, ((0, 16), (1, 8))),
        "pool_values": gaussian(seeds[4], (POOL, HEADS * HD), 1.0, 6.0, ((0, 16), (1, 8))),
        "cache_len": draw_cache_len(jax.random.fold_in(seeds[13], 71), 0),
        "cached_table": draw_cached_table(jax.random.fold_in(seeds[13], 71), 0),
        "free_blocks": draw_free_blocks(jax.random.fold_in(seeds[13], 71), 0),
        "residual_in": draw_residual_in(jax.random.fold_in(seeds[13], 71), 0),
        "out_weight": gaussian(seeds[9], (HEADS * HD, D), 0.4, 2.390625, ((0, 8),)),
        "out_bias": gaussian(seeds[10], (D,), 0.5, 3.0, ((0, 8),), jnp.float32),
        "ln_gain": jnp.clip(1.0 + 0.18 * jax.random.normal(seeds[11], (D,), jnp.float32), 0.1, 1.9),
        "ln_bias": gaussian(seeds[12], (D,), 0.5, 3.0, ((0, 8),), jnp.float32),
    }


def attend_head(q_head, k_head, v_head, visible):
    scores = jnp.dot(q_head, k_head.T, preferred_element_type=jnp.float32) * HD ** (-0.5)
    scores = jnp.where(visible, scores, -1e+30)
    peak = lax.optimization_barrier(jnp.max(scores, axis=1, keepdims=True))
    weights = jnp.where(visible, jnp.exp(scores - peak), 0.0)
    total = lax.optimization_barrier(jnp.sum(weights, axis=1, keepdims=True))
    mixed = jnp.dot(weights.astype(jnp.bfloat16), v_head, preferred_element_type=jnp.float32)
    return (mixed / total).astype(jnp.bfloat16)

def reference(queries, new_keys, new_values, pool_keys, pool_values, cache_len, cached_table, free_blocks, residual_in, out_weight, out_bias, ln_gain, ln_bias):
    width = HEADS * HD
    pool_blocks = POOL // BLOCK
    targets = free_blocks.reshape(-1)
    keys_blocked = pool_keys.reshape(pool_blocks, BLOCK, width).at[targets].set(new_keys.reshape(-1, BLOCK, width))
    values_blocked = pool_values.reshape(pool_blocks, BLOCK, width).at[targets].set(new_values.reshape(-1, BLOCK, width))
    keys_out = keys_blocked.reshape(POOL, width)
    values_out = values_blocked.reshape(POOL, width)

    def one_prompt(prompt):
        table = jnp.clip(cached_table[prompt], 0, pool_blocks - 1)
        cached_keys = keys_blocked[table].reshape(CACHE_MAX, width)
        cached_values = values_blocked[table].reshape(CACHE_MAX, width)
        begin = (prompt * NEW_LEN).astype(jnp.int32)
        fresh_queries = lax.dynamic_slice_in_dim(queries, begin, NEW_LEN, 0)
        fresh_keys = lax.dynamic_slice_in_dim(new_keys, begin, NEW_LEN, 0)
        fresh_values = lax.dynamic_slice_in_dim(new_values, begin, NEW_LEN, 0)
        all_keys = jnp.concatenate([cached_keys, fresh_keys], axis=0)
        all_values = jnp.concatenate([cached_values, fresh_values], axis=0)
        places = jnp.arange(NEW_LEN, dtype=jnp.int32)
        seen_cached = jnp.broadcast_to(jnp.arange(CACHE_MAX, dtype=jnp.int32)[None, :] < cache_len[prompt], (NEW_LEN, CACHE_MAX))
        seen_fresh = places[None, :] <= places[:, None]
        visible = jnp.concatenate([seen_cached, seen_fresh], axis=1)
        length = CACHE_MAX + NEW_LEN
        q_heads = fresh_queries.reshape(NEW_LEN, HEADS, HD).transpose(1, 0, 2)
        k_heads = all_keys.reshape(length, HEADS, HD).transpose(1, 0, 2)
        v_heads = all_values.reshape(length, HEADS, HD).transpose(1, 0, 2)
        result = lax.map(lambda trio: attend_head(trio[0], trio[1], trio[2], visible), (q_heads, k_heads, v_heads))
        return result.transpose(1, 0, 2).reshape(NEW_LEN, width)
    attn = lax.map(one_prompt, jnp.arange(PROMPTS, dtype=jnp.int32)).reshape(TOKENS, width)
    group_width = width // N_HEAD
    attn_groups = attn.reshape(TOKENS, N_HEAD, group_width).transpose(1, 0, 2)
    weight_groups = out_weight.reshape(N_HEAD, group_width, D)

    def add_group(running, pair):
        rounded = jnp.dot(pair[0], pair[1], preferred_element_type=jnp.float32).astype(jnp.bfloat16)
        rounded = lax.optimization_barrier(rounded)
        return (running + rounded.astype(jnp.float32), None)
    summed, _ = lax.scan(add_group, jnp.zeros((TOKENS, D), jnp.float32), (attn_groups, weight_groups))
    stream = residual_in.astype(jnp.float32) + summed + out_bias[None, :]
    mean = lax.optimization_barrier(jnp.mean(stream, axis=1, keepdims=True))
    centred = stream - mean
    variance = lax.optimization_barrier(jnp.mean(centred * centred, axis=1, keepdims=True))
    normed = (centred * lax.rsqrt(variance + 1e-05) * ln_gain[None, :] + ln_bias[None, :]).astype(jnp.bfloat16)
    return (stream.astype(jnp.bfloat16), normed, keys_out, values_out)
```

```python
import functools

import jax
import jax.numpy as jnp
import numpy as np
from jax import lax
from jax.experimental import pallas as pl
from jax.experimental.pallas import tpu as pltpu
from jax.sharding import Mesh
from jax.sharding import PartitionSpec as P

D = 7168
HD = 128
BLOCK = 128
ROWS = 512
FRESH = 4
COLS = 896
SIZES = {"zlo": 2, "yhi": 2, "ylo": 2, "core": 2, "zhi": 2, "x": 4}
SEQ = ("zlo", "yhi", "ylo", "core")
HEAD = ("zhi", "x")
SCALE2 = HD**-0.5 * 1.4426950408889634
ANY = pl.BlockSpec(memory_space=pl.ANY)
SMEM = pl.BlockSpec(memory_space=pltpu.SMEM)
VMEM = pl.BlockSpec(memory_space=pltpu.VMEM)


def move(value, flips=(), x_step=0):
    axes = tuple(flips) + (("x",) if x_step else ())
    sizes = [SIZES[a] for a in axes]
    pairs = []
    for source in range(int(np.prod(sizes))):
        place = list(np.unravel_index(source, sizes))
        for k, a in enumerate(axes):
            place[k] = (place[k] + x_step) % 4 if a == "x" else 1 - place[k]
        pairs.append((source, int(np.ravel_multi_index(place, sizes))))
    return lax.ppermute(value, axes, pairs)


RELATION = ((), ("core",), ("ylo",), ("ylo", "core"))


def places():
    z, yh, yl, c = (lax.axis_index(a) for a in SEQ)
    group_index = yl * 2 + c
    head = (yl ^ yh) * 2 + c
    return z, yh, group_index, head


def prep_kernel(free, q, nk, nv, pk, pv, ko, vo, f0, f1, f2, f3, c0, c1, c2, c3, spare, sems):
    z, yh, gi, head = places()
    seq = (z * 2 + yh) * 4 + gi
    count = jnp.int32(0)
    for lb in range(8):
        block = seq * 8 + lb
        taken = free[seq * FRESH] == block
        for k in range(1, FRESH):
            taken = taken | (free[seq * FRESH + k] == block)

        @pl.when(jnp.logical_not(taken) & (count < FRESH))
        def _():
            spare[count] = lb

        count = count + jnp.where(taken, 0, 1)
    copies = []

    def copy(source, target):
        one = pltpu.make_async_copy(source, target, sems.at[len(copies)])
        one.start()
        copies.append(one)

    for r, out in enumerate((c0, c1, c2, c3)):
        cols = pl.ds(pl.multiple_of((head ^ r) * HD, HD), HD)
        for s in range(FRESH):
            rows = pl.ds(pl.multiple_of(spare[s] * BLOCK, BLOCK), BLOCK)
            copy(pk.at[rows, cols], out.at[0, pl.ds(s * BLOCK, BLOCK)])
            copy(pv.at[rows, cols], out.at[1, pl.ds(s * BLOCK, BLOCK)])
    for r, out in enumerate((f0, f1, f2, f3)):
        cols = pl.ds(pl.multiple_of((head ^ r) * HD, HD), HD)
        for s, source in enumerate((q, nk, nv)):
            copy(source.at[:, cols], out.at[s])
    for s in range(FRESH):
        rows = pl.ds(pl.multiple_of(spare[s] * BLOCK, BLOCK), BLOCK)
        copy(pk.at[rows], ko.at[rows])
        copy(pv.at[rows], vo.at[rows])
        into = free[seq * FRESH + s] - seq * 8
        rows = pl.ds(pl.multiple_of(into * BLOCK, BLOCK), BLOCK)
        copy(nk.at[pl.ds(s * BLOCK, BLOCK)], ko.at[rows])
        copy(nv.at[pl.ds(s * BLOCK, BLOCK)], vo.at[rows])
    for one in copies:
        one.wait()


def prep(free, q, nk, nv, pk, pv):
    shape = lambda *s: jax.ShapeDtypeStruct(s, jnp.bfloat16)
    return pl.pallas_call(
        prep_kernel,
        out_shape=[shape(1024, 512)] * 2 + [shape(3, ROWS, HD)] * 4 + [shape(2, ROWS, HD)] * 4,
        in_specs=[SMEM] + [VMEM] * 5,
        out_specs=[ANY] * 10,
        scratch_shapes=[pltpu.SMEM((FRESH,), jnp.int32), pltpu.SemaphoreType.DMA((60,))],
        cost_estimate=pl.CostEstimate(flops=0, bytes_accessed=9 << 20, transcendentals=0),
        name="prep",
    )(free, q, nk, nv, pk, pv)


def softmax_step(q, k, v, state, mask=None):
    peak, total, acc = state
    s = lax.dot_general(q, k, (((1,), (1,)), ((), ())), preferred_element_type=jnp.float32)
    if mask is not None:
        s = jnp.where(mask, s, -1e30)
    new_peak = jnp.maximum(peak, jnp.max(s, axis=1, keepdims=True))
    p = jnp.exp2((s - new_peak) * SCALE2)
    fade = jnp.exp2((peak - new_peak) * SCALE2)
    total = total * fade + jnp.sum(p, axis=1, keepdims=True)
    acc = acc * fade + jnp.dot(p.astype(jnp.bfloat16), v, preferred_element_type=jnp.float32)
    return new_peak, total, acc


def attend_kernel(
    free, table, length, f0, f1, f2, f3, g0, g1, y0, y1, z0, z1, d0, d1,
    o0, o1, o2, o3, where, fresh, pool, sems,
):
    z, yh, gi, head = places()
    fresh_copies = [
        pltpu.make_async_copy(f, fresh.at[r], sems.at[r]) for r, f in enumerate((f0, f1, f2, f3))
    ]
    pool_copies = [
        pltpu.make_async_copy(p, pool.at[pl.ds(2 * n, 2)], sems.at[4 + n])
        for n, p in enumerate((g0, g1, y0, y1, z0, z1, d0, d1))
    ]
    for one in fresh_copies + pool_copies:
        one.start()
    prompt = z * 2 + yh
    blocks = length[prompt] // BLOCK

    def locate(n, carry):
        block = jnp.clip(table[prompt * 32 + n], 0, 127)
        seq = block // 8
        rank = block % 8
        for k in range(FRESH):
            rank = rank - jnp.where(free[seq * FRESH + k] < block, 1, 0)
        low = jnp.int32(0)
        for k in range(FRESH):
            low = low + jnp.where(free[seq * FRESH + k] < seq * 8, 1, 0)
        rank = jnp.clip(rank + low, 0, 3)
        sz, sy, si = seq // 8, (seq // 4) % 2, seq % 4
        far_y = sy ^ yh
        slot = ((sz ^ z) * 2 + far_y) * 4 + (si ^ gi ^ (2 * far_y))
        where[n] = slot * 4 + rank
        return carry

    lax.fori_loop(0, blocks, locate, 0)
    for one in fresh_copies + pool_copies:
        one.wait()
    rows = lax.broadcasted_iota(jnp.int32, (ROWS, ROWS), 0)
    columns = lax.broadcasted_iota(jnp.int32, (ROWS, ROWS), 1)
    causal = columns <= rows

    def block_of(n, kv):
        at = where[n]
        return pool[at // 4, kv, pl.ds(pl.multiple_of((at % 4) * BLOCK, BLOCK), BLOCK), :]

    for r, out in enumerate((o0, o1, o2, o3)):
        q = fresh[r, 0]
        state = (
            jnp.full((ROWS, 1), -1e30, jnp.float32),
            jnp.zeros((ROWS, 1), jnp.float32),
            jnp.zeros((ROWS, HD), jnp.float32),
        )
        state = softmax_step(q, fresh[r, 1], fresh[r, 2], state, causal)

        def earlier(n, state):
            slot = n ^ gi
            return softmax_step(q, fresh[slot, 1], fresh[slot, 2], state)

        state = lax.fori_loop(0, gi ^ r, earlier, state)

        def four(n, state):
            k = jnp.concatenate([block_of(n * 4 + m, 0) for m in range(4)], axis=0)
            v = jnp.concatenate([block_of(n * 4 + m, 1) for m in range(4)], axis=0)
            return softmax_step(q, k, v, state)

        state = lax.fori_loop(0, blocks // 4, four, state)

        def single(n, state):
            return softmax_step(q, block_of(n, 0), block_of(n, 1), state)

        state = lax.fori_loop(blocks // 4 * 4, blocks, single, state)
        out[...] = (state[2] / state[1]).astype(jnp.bfloat16)


def attention(free, table, length, fresh, pools):
    return pl.pallas_call(
        attend_kernel,
        out_shape=[jax.ShapeDtypeStruct((ROWS, HD), jnp.bfloat16)] * 4,
        in_specs=[SMEM] * 3 + [ANY] * 12,
        out_specs=[VMEM] * 4,
        scratch_shapes=[
            pltpu.SMEM((32,), jnp.int32),
            pltpu.VMEM((4, 3, ROWS, HD), jnp.bfloat16),
            pltpu.VMEM((16, 2, ROWS, HD), jnp.bfloat16),
            pltpu.SemaphoreType.DMA((12,)),
        ],
        cost_estimate=pl.CostEstimate(
            flops=11_000_000 * 512, bytes_accessed=7 << 20, transcendentals=11_000_000
        ),
        name="attend",
    )(free, table, length, *fresh, *pools)


def project_kernel(far, a0, ap, am, a2a, a2b, w, wp, wm, w2, out, at, wt, sems):
    _, _, _, head = places()
    zh, x = lax.axis_index("zhi"), lax.axis_index("x")
    half = zh ^ far
    copies = []

    def copy(source, target):
        one = pltpu.make_async_copy(source, target, sems.at[len(copies)])
        one.start()
        copies.append(one)

    for n, (source, r0) in enumerate(((a0, 0), (ap, 0), (am, 0), (a2a, 0), (a2b, 2))):
        for r in range(source.shape[0]):
            col = min(n, 3) * 512 + (head ^ (r0 + r)) * HD
            copy(source.at[r], at.at[:, pl.ds(pl.multiple_of(col, HD), HD)])
    cols = pl.ds(pl.multiple_of((half * 4 + x) * COLS, HD), COLS)
    copy(w.at[:, cols], wt.at[pl.ds(0, 512)])
    for n, source in enumerate((wp, wm, w2)):
        copy(source.at[half], wt.at[pl.ds(512 * (n + 1), 512)])
    for one in copies:
        one.wait()

    def tile(n, carry):
        rows = pl.ds(pl.multiple_of(n * 128, 128), 128)
        out[rows, :] = jnp.dot(
            at[rows, :], wt[...], preferred_element_type=jnp.float32
        ).astype(out.dtype)
        return carry

    lax.fori_loop(0, ROWS // 128, tile, 0)


def project(far, dtype, pieces, weights):
    return pl.pallas_call(
        functools.partial(project_kernel, far),
        out_shape=jax.ShapeDtypeStruct((ROWS, COLS), dtype),
        in_specs=[ANY] * 9,
        out_specs=VMEM,
        scratch_shapes=[
            pltpu.VMEM((ROWS, 2048), jnp.bfloat16),
            pltpu.VMEM((2048, COLS), jnp.bfloat16),
            pltpu.SemaphoreType.DMA((20,)),
        ],
        cost_estimate=pl.CostEstimate(
            flops=2 * ROWS * 2048 * COLS, bytes_accessed=7 << 20, transcendentals=0
        ),
        name="project_far" if far else "project_near",
    )(*pieces, *weights)


def merge(stats, count):
    mean = sum(s[0] for s in stats) / len(stats)
    square = sum(s[1] + count * jnp.square(s[0] - mean) for s in stats)
    return jnp.stack([mean, square])


def shards(
    queries, new_keys, new_values, pool_keys, pool_values, cache_len, cached_table, free_blocks,
    residual_in, out_weight, out_bias, ln_gain, ln_bias,
):
    free = free_blocks.reshape(-1)
    table = cached_table.reshape(-1)
    out = prep(free, queries, new_keys, new_values, pool_keys, pool_values)
    keys_out, values_out, fresh, cached = out[0], out[1], out[2:6], out[6:10]

    got = [cached[0]] + [move(cached[r], RELATION[r]) for r in (1, 2, 3)]
    g0, g1 = jnp.stack(got[:2]), jnp.stack(got[2:])
    flat = lambda v: v.reshape(-1, *v.shape[2:]) if v.ndim > 4 else v
    y0, z0 = move(g0, ("yhi", "ylo")), move(g0, ("zlo",))
    y1, z1 = move(g1, ("yhi", "ylo")), move(g1, ("zlo",))
    d0, d1 = move(y0, ("zlo",)), move(z1, ("yhi", "ylo"))
    fresh = [fresh[0]] + [move(fresh[r], RELATION[r]) for r in (1, 2, 3)]

    core, x = lax.axis_index("core"), lax.axis_index("x")

    def weight_part(step):
        col = (core * 4 + (x + step) % 4) * COLS
        part = move(lax.dynamic_slice(out_weight, (0, col), (512, COLS)), (), step)
        other = move(part, ("core",))
        first = jnp.where(core == 0, part, other)
        second = jnp.where(core == 0, other, part)
        return jnp.stack([first, second])

    weights = [out_weight] + [weight_part(step) for step in (1, 3, 2)]

    o = attention(free, table, cache_len, fresh, (g0, g1, y0, y1, z0, z1, d0, d1))
    a0 = jnp.stack([o[0]] + [move(o[r], RELATION[r]) for r in (1, 2, 3)])
    ap, am = move(a0, (), 1), move(a0, (), 3)
    pieces = (a0, ap, am, move(ap[:2], (), 1), move(am[2:], (), 3))
    sent = move(project(1, jnp.bfloat16, pieces, weights), ("zhi",))
    near = project(0, jnp.float32, pieces, weights)
    stream = (
        residual_in.astype(jnp.float32) + near + sent.astype(jnp.float32) + out_bias[None, :]
    )
    mean = jnp.sum(stream, axis=1) / COLS
    square = jnp.sum(jnp.square(stream - mean[:, None]), axis=1)
    stats = jnp.stack([mean, square])
    stats = merge([stats] + [move(stats, (), k) for k in (1, 2, 3)], COLS)
    stats = merge([stats, move(stats, ("zhi",))], 4 * COLS)
    mean, variance = stats[0], stats[1] / D
    normed = (
        (stream - mean[:, None]) * lax.rsqrt(variance[:, None] + 1e-05) * ln_gain[None, :]
        + ln_bias[None, :]
    ).astype(jnp.bfloat16)
    return (stream.astype(jnp.bfloat16), normed, keys_out, values_out)


def solution(mesh):
    fine = Mesh(mesh.devices.reshape(tuple(SIZES.values())), tuple(SIZES))
    both = P(SEQ, HEAD)
    head = P(HEAD)
    in_specs = (both,) * 5 + (P(), P(), P()) + (both, P(HEAD, None), head, head, head)
    return jax.shard_map(
        shards, mesh=fine, in_specs=in_specs, out_specs=(both,) * 4, check_vma=False
    )
```

```python
import functools

import jax
import jax.numpy as jnp
import numpy as np
from jax import lax
from jax.experimental import pallas as pl
from jax.experimental.pallas import tpu as pltpu
from jax.sharding import Mesh
from jax.sharding import PartitionSpec as P

D = 7168
HD = 128
BLOCK = 128
ROWS = 512
HALF = 256
FRESH = 4
COLS = 896
SIZES = {"zlo": 2, "yhi": 2, "ylo": 2, "core": 2, "zhi": 2, "x": 4}
SEQ = ("zlo", "yhi", "ylo", "core")
HEAD = ("zhi", "x")
SCALE2 = HD**-0.5 * 1.4426950408889634
ANY = pl.BlockSpec(memory_space=pl.ANY)
SMEM = pl.BlockSpec(memory_space=pltpu.SMEM)
VMEM = pl.BlockSpec(memory_space=pltpu.VMEM)


def move(value, flips=(), x_step=0):
    axes = tuple(flips) + (("x",) if x_step else ())
    sizes = [SIZES[a] for a in axes]
    pairs = []
    for source in range(int(np.prod(sizes))):
        place = list(np.unravel_index(source, sizes))
        for k, a in enumerate(axes):
            place[k] = (place[k] + x_step) % 4 if a == "x" else 1 - place[k]
        pairs.append((source, int(np.ravel_multi_index(place, sizes))))
    return lax.ppermute(value, axes, pairs)


RELATION = ((), ("core",), ("ylo",), ("ylo", "core"))


def places():
    z, yh, yl, c = (lax.axis_index(a) for a in SEQ)
    group_index = yl * 2 + c
    head = (yl ^ yh) * 2 + c
    return z, yh, group_index, head


def prep_kernel(free, q, nk, nv, pk, pv, ko, vo, fq, f0, f1, fy, c0, c1, cy, spare, sems):
    z, yh, gi, head = places()
    seq = (z * 2 + yh) * 4 + gi
    count = jnp.int32(0)
    for lb in range(8):
        block = seq * 8 + lb
        taken = free[seq * FRESH] == block
        for k in range(1, FRESH):
            taken = taken | (free[seq * FRESH + k] == block)

        @pl.when(jnp.logical_not(taken) & (count < FRESH))
        def _():
            spare[count] = lb

        count = count + jnp.where(taken, 0, 1)
    copies = []

    def copy(source, target):
        one = pltpu.make_async_copy(source, target, sems.at[len(copies)])
        one.start()
        copies.append(one)

    for r, out in ((2, cy.at[0]), (3, cy.at[1]), (1, c1), (0, c0)):
        cols = pl.ds(pl.multiple_of((head ^ r) * HD, HD), HD)
        for s in range(FRESH):
            rows = pl.ds(pl.multiple_of(spare[s] * BLOCK, BLOCK), BLOCK)
            copy(pk.at[rows, cols], out.at[0, pl.ds(s * BLOCK, BLOCK)])
            copy(pv.at[rows, cols], out.at[1, pl.ds(s * BLOCK, BLOCK)])
    for r, out in ((2, fy.at[0]), (3, fy.at[1]), (1, f1), (0, f0)):
        cols = pl.ds(pl.multiple_of((head ^ r) * HD, HD), HD)
        for s, source in enumerate((nk, nv)):
            copy(source.at[:, cols], out.at[s])
    for k in range(4):
        cols = pl.ds(pl.multiple_of((k ^ (2 * yh)) * HD, HD), HD)
        copy(q.at[:, cols], fq.at[k])
    for s in range(FRESH):
        rows = pl.ds(pl.multiple_of(spare[s] * BLOCK, BLOCK), BLOCK)
        copy(pk.at[rows], ko.at[rows])
        copy(pv.at[rows], vo.at[rows])
        into = jnp.clip(free[seq * FRESH + s] - seq * 8, 0, 7)
        rows = pl.ds(pl.multiple_of(into * BLOCK, BLOCK), BLOCK)
        copy(nk.at[pl.ds(s * BLOCK, BLOCK)], ko.at[rows])
        copy(nv.at[pl.ds(s * BLOCK, BLOCK)], vo.at[rows])
    for one in copies:
        one.wait()


def prep(free, q, nk, nv, pk, pv):
    shape = lambda *s: jax.ShapeDtypeStruct(s, jnp.bfloat16)
    return pl.pallas_call(
        prep_kernel,
        out_shape=[shape(1024, 512)] * 2
        + [shape(4, ROWS, HD)]
        + ([shape(2, ROWS, HD)] * 2 + [shape(2, 2, ROWS, HD)]) * 2,
        in_specs=[SMEM] + [VMEM] * 5,
        out_specs=[ANY] * 9,
        scratch_shapes=[pltpu.SMEM((FRESH,), jnp.int32), pltpu.SemaphoreType.DMA((60,))],
        cost_estimate=pl.CostEstimate(flops=0, bytes_accessed=9 << 20, transcendentals=0),
        name="prep",
    )(free, q, nk, nv, pk, pv)


def softmax_step(q, k, v, state, mask=None):
    peak, total, acc = state
    s = lax.dot_general(k, q, (((1,), (1,)), ((), ())), preferred_element_type=jnp.float32)
    if mask is not None:
        s = jnp.where(mask, s, -1e30)
    new_peak = jnp.maximum(peak, jnp.max(s, axis=0, keepdims=True))
    p = jnp.exp2((s - new_peak) * SCALE2)
    fade = jnp.exp2((peak - new_peak) * SCALE2)
    total = total * fade + jnp.sum(p, axis=0, keepdims=True)
    acc = acc * fade + lax.dot_general(
        v, p.astype(jnp.bfloat16), (((0,), (0,)), ((), ())), preferred_element_type=jnp.float32
    )
    return new_peak, total, acc


def locate_kernel(free, table, length, early, late):
    z, yh, gi, _ = places()
    prompt = z * 2 + yh

    def one(n, counts):
        block = jnp.clip(table[prompt * 32 + n], 0, 127)
        seq = block // 8
        rank = block % 8
        for k in range(FRESH):
            rank = rank - jnp.where(free[seq * FRESH + k] < block, 1, 0)
        rank = jnp.clip(rank, 0, FRESH - 1)
        far_z, far_y = (seq // 8) ^ z, ((seq // 4) % 2) ^ yh
        group = far_z * 2 + far_y
        r = (seq % 4) ^ gi ^ (2 * far_y)
        is_late = jnp.where((group == 3) | ((group > 0) & (r > 1)), 1, 0)
        early[1 + counts[0]] = (
            jnp.clip(jnp.where(group == 0, r, 2 + 2 * group + r), 0, 7) * FRESH + rank
        )
        late[1 + counts[1]] = (
            jnp.clip(jnp.where(group == 3, 4 + r, 2 * group + r - 4), 0, 7) * FRESH + rank
        )
        return counts[0] + 1 - is_late, counts[1] + is_late

    counts = lax.fori_loop(0, length[prompt] // BLOCK, one, (jnp.int32(0), jnp.int32(0)))
    early[0] = counts[0]
    late[0] = counts[1]


def locate(free, table, length):
    return pl.pallas_call(
        locate_kernel,
        out_shape=[jax.ShapeDtypeStruct((40,), jnp.int32)] * 2,
        in_specs=[SMEM] * 3,
        out_specs=[SMEM] * 2,
        cost_estimate=pl.CostEstimate(flops=0, bytes_accessed=4 << 20, transcendentals=0),
        name="locate",
    )(free, table, length)


def cut_kernel(gate, weight, out, buf, sems):
    core = lax.axis_index("core")
    reads, writes = [], []
    for n in range(4):
        cols = pl.ds(pl.multiple_of((core * 4 + n) * COLS, HD), COLS)
        reads.append(pltpu.make_async_copy(weight.at[:, cols], buf.at[n], sems.at[n]))
        writes.append(pltpu.make_async_copy(buf.at[n], out.at[n], sems.at[4 + n]))
        reads[-1].start()
    for read, write in zip(reads, writes):
        read.wait()
        write.start()
    for write in writes:
        write.wait()


def cut(gate, weight):
    return pl.pallas_call(
        cut_kernel,
        out_shape=jax.ShapeDtypeStruct((4, 512, COLS), jnp.bfloat16),
        in_specs=[SMEM, ANY],
        out_specs=ANY,
        scratch_shapes=[
            pltpu.VMEM((4, 512, COLS), jnp.bfloat16),
            pltpu.SemaphoreType.DMA((8,)),
        ],
        cost_estimate=pl.CostEstimate(flops=0, bytes_accessed=7 << 20, transcendentals=0),
        name="cut",
    )(gate, weight)


def pool_steps(q, blocks, pool, state):
    count = blocks[0]

    def block_of(n, kv):
        at = blocks[1 + n]
        rows = pl.ds(pl.multiple_of((at % FRESH) * BLOCK, BLOCK), BLOCK)
        return pool[at // FRESH, kv, rows, :]

    def group(first, width, state, masked):
        at = [first + m for m in range(width)]
        mask = None
        if masked:
            row = lax.broadcasted_iota(jnp.int32, (width * BLOCK, q.shape[0]), 0)
            mask = row < (count - first) * BLOCK
            at = [jnp.minimum(a, count - 1) for a in at]
        k = jnp.concatenate([block_of(a, 0) for a in at], axis=0)
        v = jnp.concatenate([block_of(a, 1) for a in at], axis=0)
        return softmax_step(q, k, v, state, mask)

    wide = count // 8
    state = lax.fori_loop(0, wide, lambda n, s: group(n * 8, 8, s, False), state)
    rest = (count - wide * 8 + 3) // 4
    return lax.fori_loop(0, rest, lambda n, s: group(wide * 8 + n * 4, 4, s, True), state)


STATE = [
    jax.ShapeDtypeStruct((HD, 4 * ROWS), jnp.float32),
    jax.ShapeDtypeStruct((8, 4 * ROWS), jnp.float32),
]


def early_kernel(blocks, fq, g0, g1, y0, z0, acc_out, row_out, pool, sems):
    copies = [
        pltpu.make_async_copy(p, pool.at[pl.ds(2 * n, 2)], sems.at[n])
        for n, p in enumerate((g0, g1, y0, z0))
    ]
    for one in copies:
        one.start()
    for one in copies:
        one.wait()
    n = 4 * ROWS
    state = (
        jnp.full((1, n), -1e30, jnp.float32),
        jnp.zeros((1, n), jnp.float32),
        jnp.zeros((HD, n), jnp.float32),
    )
    state = pool_steps(fq[...].reshape(n, HD), blocks, pool, state)
    row_out[0:1, :] = state[0]
    row_out[1:2, :] = state[1]
    acc_out[...] = state[2]


def attend_early(blocks, fq, pools):
    return pl.pallas_call(
        early_kernel,
        out_shape=STATE,
        in_specs=[SMEM, VMEM] + [ANY] * 4,
        out_specs=[VMEM] * 2,
        scratch_shapes=[
            pltpu.VMEM((8, 2, ROWS, HD), jnp.bfloat16),
            pltpu.SemaphoreType.DMA((4,)),
        ],
        cost_estimate=pl.CostEstimate(
            flops=4_000_000 * 512, bytes_accessed=4 << 20, transcendentals=4_000_000
        ),
        name="attend_early",
    )(blocks, fq, *pools)


def fresh_kernel(fq, f0, f1, fy, f3, acc, row, acc_out, row_out, fresh, sems):
    _, _, gi, _ = places()
    copies = [
        pltpu.make_async_copy(f, fresh.at[gi ^ r], sems.at[r])
        for r, f in enumerate((f0, f1, fy.at[0], f3))
    ]
    for one in copies:
        one.start()
    acc_out[...] = acc[...]
    row_out[...] = row[...]
    for one in copies:
        one.wait()
    for k in range(4):
        n = (4 - k) * ROWS
        cols = pl.ds(k * ROWS, n)
        key = lax.broadcasted_iota(jnp.int32, (ROWS, n), 0)
        query = lax.broadcasted_iota(jnp.int32, (ROWS, n), 1)
        state = (row_out[0:1, cols], row_out[1:2, cols], acc_out[:, cols])
        q = fq[k:].reshape(n, HD)
        state = softmax_step(q, fresh[k, 0], fresh[k, 1], state, key <= query)
        row_out[0:1, cols] = state[0]
        row_out[1:2, cols] = state[1]
        acc_out[:, cols] = state[2]


def attend_fresh(fq, fresh, acc, row):
    return pl.pallas_call(
        fresh_kernel,
        out_shape=STATE,
        in_specs=[VMEM] + [ANY] * 4 + [VMEM] * 2,
        out_specs=[VMEM] * 2,
        scratch_shapes=[
            pltpu.VMEM((4, 2, ROWS, HD), jnp.bfloat16),
            pltpu.SemaphoreType.DMA((4,)),
        ],
        cost_estimate=pl.CostEstimate(
            flops=2_600_000 * 512, bytes_accessed=4 << 20, transcendentals=2_600_000
        ),
        name="attend_fresh",
    )(fq, *fresh, acc, row)


def late_kernel(blocks, fq, y1, z1, d0, d1, acc, row, out0, out1, pool, sems):
    _, _, gi, _ = places()
    copies = [
        pltpu.make_async_copy(p, pool.at[pl.ds(2 * n, 2)], sems.at[n])
        for n, p in enumerate((y1, z1, d0, d1))
    ]
    for one in copies:
        one.start()
    for one in copies:
        one.wait()
    state = (row[0:1, :], row[1:2, :], acc[...])
    _, total, mixed = pool_steps(fq[...].reshape(4 * ROWS, HD), blocks, pool, state)
    mixed = mixed / total
    for k in range(4):
        part = mixed[:, k * ROWS : (k + 1) * ROWS].T.astype(jnp.bfloat16)
        out0[k ^ gi] = part[:HALF]
        out1[k] = part[HALF:]


def attend_late(blocks, fq, pools, acc, row):
    return pl.pallas_call(
        late_kernel,
        out_shape=[jax.ShapeDtypeStruct((4, HALF, HD), jnp.bfloat16)] * 2,
        in_specs=[SMEM, VMEM] + [ANY] * 4 + [VMEM] * 2,
        out_specs=[VMEM] * 2,
        scratch_shapes=[
            pltpu.VMEM((8, 2, ROWS, HD), jnp.bfloat16),
            pltpu.SemaphoreType.DMA((4,)),
        ],
        cost_estimate=pl.CostEstimate(
            flops=4_000_000 * 512, bytes_accessed=4 << 20, transcendentals=4_000_000
        ),
        name="attend_late",
    )(blocks, fq, *pools, acc, row)


def project_kernel(far, ordered, a0, ap, am, a2a, a2b, mine, other, out, at, wt, sems):
    core = lax.axis_index("core")
    _, yh, _, head = places()
    head = 2 * yh if ordered else head
    x = lax.axis_index("x")
    half = lax.axis_index("zhi") ^ far
    copies = []

    def copy(source, target):
        one = pltpu.make_async_copy(source, target, sems.at[len(copies)])
        one.start()
        copies.append(one)

    for n in range(4):
        target = wt.at[pl.ds(512 * n, 512)]
        one = pltpu.make_async_copy(mine.at[n], target, sems.at[n])
        two = pltpu.make_async_copy(other.at[n], target, sems.at[n])
        pl.when(half == core)(one.start)
        pl.when(half != core)(two.start)
        copies.append(one)
    for source, step, k0 in ((a0, 0, 0), (ap, 3, 0), (am, 1, 0), (a2a, 2, 0), (a2b, 2, 2)):
        for k in range(source.shape[0]):
            col = ((x + step) % 4) * 512 + (head ^ (k0 + k)) * HD
            copy(source.at[k], at.at[:, pl.ds(pl.multiple_of(col, HD), HD)])
    for one in copies:
        one.wait()

    def tile(n, carry):
        rows = pl.ds(pl.multiple_of(n * 128, 128), 128)
        out[rows, :] = jnp.dot(
            at[rows, :], wt[...], preferred_element_type=jnp.float32
        ).astype(out.dtype)
        return carry

    lax.fori_loop(0, HALF // 128, tile, 0)


def project(far, ordered, dtype, pieces, weights):
    return pl.pallas_call(
        functools.partial(project_kernel, far, ordered),
        out_shape=jax.ShapeDtypeStruct((HALF, COLS), dtype),
        in_specs=[ANY] * 7,
        out_specs=VMEM,
        scratch_shapes=[
            pltpu.VMEM((HALF, 2048), jnp.bfloat16),
            pltpu.VMEM((2048, COLS), jnp.bfloat16),
            pltpu.SemaphoreType.DMA((20,)),
        ],
        cost_estimate=pl.CostEstimate(
            flops=2 * HALF * 2048 * COLS, bytes_accessed=5 << 20, transcendentals=0
        ),
        name=f"project{ordered}_" + ("far" if far else "near"),
    )(*pieces, *weights)


def merge(stats, count):
    mean = sum(s[0] for s in stats) / len(stats)
    square = sum(s[1] + count * jnp.square(s[0] - mean) for s in stats)
    return jnp.stack([mean, square])


def shards(
    queries, new_keys, new_values, pool_keys, pool_values, cache_len, cached_table, free_blocks,
    residual_in, out_weight, out_bias, ln_gain, ln_bias,
):
    free = free_blocks.reshape(-1)
    table = cached_table.reshape(-1)
    out = prep(free, queries, new_keys, new_values, pool_keys, pool_values)
    keys_out, values_out, fq, f0, f1, fy, c0, c1, cy = out
    after = lambda value, *others: lax.optimization_barrier((value, *others))[0]
    group = ("ylo", "core")

    fq = lax.all_to_all(fq, group, 0, 0)
    cy = move(cy, ("ylo",))
    g0 = jnp.stack([c0, move(c1, ("core",))])
    y0, z0 = move(g0, ("yhi", "ylo")), move(g0, ("zlo",))
    early, late = locate(free, table, cache_len)

    g1 = after(jnp.stack([cy[0], move(cy[1], ("core",))]), y0, z0)
    y1, z1 = move(g1, ("yhi", "ylo")), move(g1, ("zlo",))
    d0 = move(after(y0, g1), ("zlo",))
    fy = move(after(fy, g1), ("ylo",))
    f1 = move(after(f1, g1), ("core",))
    f3 = move(fy[1], ("core",))

    part = cut(after(jnp.zeros((1,), jnp.int32), g1, fq), out_weight)
    mine = lax.all_to_all(part, "x", 0, 0)

    acc, row = attend_early(early, fq, (g0, g1, y0, z0))
    d1 = move(after(z1, acc), ("yhi", "ylo"))
    acc, row = attend_fresh(fq, (f0, f1, fy, f3), after(acc, y1), row)
    mixed0, mixed1 = attend_late(late, fq, (y1, z1, d0, d1), acc, row)
    other = move(after(mine, mixed0), ("core",))

    sums = []
    for ordered, o in enumerate((mixed0, mixed1)):
        if ordered:
            a0 = lax.all_to_all(o, group, 0, 0)
        else:
            a0 = jnp.stack([o[0]] + [move(o[r], RELATION[r]) for r in (1, 2, 3)])
        ap, am = move(a0, (), 1), move(a0, (), 3)
        pieces = (a0, ap, am, move(ap[:2], (), 1), move(am[2:], (), 3))
        sent = move(project(1, ordered, jnp.bfloat16, pieces, (mine, other)), ("zhi",))
        near = project(0, ordered, jnp.float32, pieces, (mine, other))
        sums.append(near + sent.astype(jnp.float32))
    stream = (
        residual_in.astype(jnp.float32) + jnp.concatenate(sums, axis=0) + out_bias[None, :]
    )
    mean = jnp.sum(stream, axis=1) / COLS
    square = jnp.sum(jnp.square(stream - mean[:, None]), axis=1)
    stats = jnp.stack([mean, square])
    stats = merge([stats] + [move(stats, (), k) for k in (1, 2, 3)], COLS)
    stats = merge([stats, move(stats, ("zhi",))], 4 * COLS)
    mean, variance = stats[0], stats[1] / D
    normed = (
        (stream - mean[:, None]) * lax.rsqrt(variance[:, None] + 1e-05) * ln_gain[None, :]
        + ln_bias[None, :]
    ).astype(jnp.bfloat16)
    return (stream.astype(jnp.bfloat16), normed, keys_out, values_out)


def solution(mesh):
    fine = Mesh(mesh.devices.reshape(tuple(SIZES.values())), tuple(SIZES))
    both = P(SEQ, HEAD)
    head = P(HEAD)
    in_specs = (both,) * 5 + (P(), P(), P()) + (both, P(HEAD, None), head, head, head)
    return jax.shard_map(
        shards, mesh=fine, in_specs=in_specs, out_specs=(both,) * 4, check_vma=False
    )
```

```python
import functools

import jax
import jax.numpy as jnp
import numpy as np
from jax import lax
from jax.experimental import pallas as pl
from jax.experimental.pallas import tpu as pltpu
from jax.sharding import Mesh
from jax.sharding import PartitionSpec as P

D = 7168
HD = 128
BLOCK = 128
ROWS = 512
HALF = 256
FRESH = 4
COLS = 896
SIZES = {"zlo": 2, "yhi": 2, "ylo": 2, "core": 2, "zhi": 2, "x": 4}
SEQ = ("zlo", "yhi", "ylo", "core")
HEAD = ("zhi", "x")
SCALE2 = HD**-0.5 * 1.4426950408889634
ANY = pl.BlockSpec(memory_space=pl.ANY)
SMEM = pl.BlockSpec(memory_space=pltpu.SMEM)
VMEM = pl.BlockSpec(memory_space=pltpu.VMEM)


def move(value, flips=(), x_step=0):
    axes = tuple(flips) + (("x",) if x_step else ())
    sizes = [SIZES[a] for a in axes]
    pairs = []
    for source in range(int(np.prod(sizes))):
        place = list(np.unravel_index(source, sizes))
        for k, a in enumerate(axes):
            place[k] = (place[k] + x_step) % 4 if a == "x" else 1 - place[k]
        pairs.append((source, int(np.ravel_multi_index(place, sizes))))
    return lax.ppermute(value, axes, pairs)


RELATION = ((), ("core",), ("ylo",), ("ylo", "core"))


def places():
    z, yh, yl, c = (lax.axis_index(a) for a in SEQ)
    group_index = yl * 2 + c
    head = (yl ^ yh) * 2 + c
    return z, yh, group_index, head


def find_spare(free, spare):
    z, yh, gi, _ = places()
    prompt = z * 2 + yh
    count = jnp.int32(0)
    for lb in range(8):
        block = (prompt * 4 + gi) * 8 + lb
        taken = free[prompt, gi * FRESH] == block
        for k in range(1, FRESH):
            taken = taken | (free[prompt, gi * FRESH + k] == block)

        @pl.when(jnp.logical_not(taken) & (count < FRESH))
        def _():
            spare[count] = lb

        count = count + jnp.where(taken, 0, 1)


class Copies:
    def __init__(self, sems):
        self.sems, self.open, self.used = sems, [], 0

    def start(self, source, target):
        one = pltpu.make_async_copy(source, target, self.sems.at[self.used])
        self.used += 1
        one.start()
        self.open.append(one)
        return one

    def wait(self):
        for one in self.open:
            one.wait()
        self.open = []


def rows_of(block):
    return pl.ds(pl.multiple_of(block * BLOCK, BLOCK), BLOCK)


def cols_of(head):
    return pl.ds(pl.multiple_of(head * HD, HD), HD)


def prep_kernel(free, q, pk, pv, fq, c0, c1, cy, spare, held, held_q, sems):
    _, yh, _, head = places()
    copies = Copies(sems)
    query = pltpu.make_async_copy(q, held_q, sems.at[sems.shape[0] - 1])
    query.start()
    find_spare(free, spare)
    for s in range(FRESH):
        for kv, source in enumerate((pk, pv)):
            copies.start(source.at[rows_of(spare[s])], held.at[kv, pl.ds(s * BLOCK, BLOCK)])
    copies.wait()
    for r, out in ((1, c1), (2, cy.at[0]), (3, cy.at[1]), (0, c0)):
        for kv in range(2):
            copies.start(held.at[kv, :, cols_of(head ^ r)], out.at[kv])
    query.wait()
    for k in range(4):
        copies.start(held_q.at[:, cols_of(k ^ (2 * yh))], fq.at[k])
    copies.wait()


def prep(free, q, pk, pv):
    shape = lambda *s: jax.ShapeDtypeStruct(s, jnp.bfloat16)
    return pl.pallas_call(
        prep_kernel,
        out_shape=[shape(4, ROWS, HD)] + [shape(2, ROWS, HD)] * 2 + [shape(2, 2, ROWS, HD)],
        in_specs=[SMEM] + [ANY] * 3,
        out_specs=[ANY] * 4,
        scratch_shapes=[
            pltpu.SMEM((FRESH,), jnp.int32),
            pltpu.VMEM((2, ROWS, 512), jnp.bfloat16),
            pltpu.VMEM((ROWS, 512), jnp.bfloat16),
            pltpu.SemaphoreType.DMA((24,)),
        ],
        cost_estimate=pl.CostEstimate(flops=0, bytes_accessed=4 << 20, transcendentals=0),
        name="prep",
    )(free, q, pk, pv)


def side_kernel(
    gate, free, table, length, nk, nv, pk, pv, weight,
    cut, ko, vo, f0, f1, fy, early, mid, late, spare, wide, new, old, sems,
):
    z, yh, gi, head = places()
    core = lax.axis_index("core")
    prompt = z * 2 + yh
    copies = Copies(sems)
    reads = [
        copies.start(weight.at[:, pl.ds(pl.multiple_of((core * 4 + n) * COLS, HD), COLS)], wide.at[n])
        for n in range(4)
    ]
    for kv, source in enumerate((nk, nv)):
        copies.start(source, new.at[kv])
    find_spare(free, spare)
    for s in range(FRESH):
        for kv, source in enumerate((pk, pv)):
            copies.start(source.at[rows_of(spare[s])], old.at[kv, pl.ds(s * BLOCK, BLOCK)])

    def one(n, counts):
        block = jnp.clip(table[prompt, n], 0, 127)
        owner, place = block // 32, (block // 8) % 4
        rank = block % 8
        for k in range(FRESH):
            rank = rank - jnp.where(free[owner, place * FRESH + k] < block, 1, 0)
        rank = jnp.clip(rank, 0, FRESH - 1)
        far_y = (owner % 2) ^ yh
        group = ((owner // 2) ^ z) * 2 + far_y
        r = place ^ gi ^ (2 * far_y)
        is_late = jnp.where(group == 3, 1, 0)
        is_mid = jnp.where((group > 0) & (group < 3) & (r > 1), 1, 0)
        early[1 + counts[0]] = (
            jnp.clip(jnp.where(group == 0, r, 2 + 2 * group + r), 0, 7) * FRESH + rank
        )
        mid[1 + counts[1]] = jnp.clip(2 * group + r - 4, 0, 3) * FRESH + rank
        late[1 + counts[2]] = r * FRESH + rank
        return counts[0] + 1 - is_late - is_mid, counts[1] + is_mid, counts[2] + is_late

    counts = lax.fori_loop(0, length[prompt] // BLOCK, one, (jnp.int32(0),) * 3)
    for listed, count in zip((early, mid, late), counts):
        listed[0] = count
    copies.wait()
    for n in range(4):
        copies.start(wide.at[n], cut.at[n])
    for kv, out in enumerate((ko, vo)):
        for r, target in ((2, fy.at[0]), (3, fy.at[1]), (1, f1), (0, f0)):
            copies.start(new.at[kv, :, cols_of(head ^ r)], target.at[kv])
        for s in range(FRESH):
            rows = pl.ds(s * BLOCK, BLOCK)
            into = jnp.clip(free[prompt, gi * FRESH + s] - (prompt * 4 + gi) * 8, 0, 7)
            copies.start(new.at[kv, rows], out.at[rows_of(into)])
            copies.start(old.at[kv, rows], out.at[rows_of(spare[s])])
    copies.wait()


def side(gate, free, table, length, nk, nv, pk, pv, weight):
    shape = lambda *s: jax.ShapeDtypeStruct(s, jnp.bfloat16)
    return pl.pallas_call(
        side_kernel,
        out_shape=[shape(4, 512, COLS)]
        + [shape(1024, 512)] * 2
        + [shape(2, ROWS, HD)] * 2
        + [shape(2, 2, ROWS, HD)]
        + [jax.ShapeDtypeStruct((40,), jnp.int32)] * 3,
        in_specs=[SMEM] * 4 + [ANY] * 5,
        out_specs=[ANY] * 6 + [SMEM] * 3,
        scratch_shapes=[
            pltpu.SMEM((FRESH,), jnp.int32),
            pltpu.VMEM((4, 512, COLS), jnp.bfloat16),
            pltpu.VMEM((2, ROWS, 512), jnp.bfloat16),
            pltpu.VMEM((2, ROWS, 512), jnp.bfloat16),
            pltpu.SemaphoreType.DMA((48,)),
        ],
        cost_estimate=pl.CostEstimate(flops=0, bytes_accessed=14 << 20, transcendentals=0),
        name="side",
    )(gate, free, table, length, nk, nv, pk, pv, weight)


def softmax_step(q, k, v, state, mask=None):
    peak, total, acc = state
    s = lax.dot_general(k, q, (((1,), (1,)), ((), ())), preferred_element_type=jnp.float32)
    if mask is not None:
        s = jnp.where(mask, s, -1e30)
    new_peak = jnp.maximum(peak, jnp.max(s, axis=0, keepdims=True))
    p = jnp.exp2((s - new_peak) * SCALE2)
    fade = jnp.exp2((peak - new_peak) * SCALE2)
    total = total * fade + jnp.sum(p, axis=0, keepdims=True)
    acc = acc * fade + lax.dot_general(
        v, p.astype(jnp.bfloat16), (((0,), (0,)), ((), ())), preferred_element_type=jnp.float32
    )
    return new_peak, total, acc


def pool_steps(queries, blocks, pool, acc, row):
    count = blocks[0]

    def group(first, width, q, cols, masked):
        at = [first + m for m in range(width)]
        mask = None
        if masked:
            key = lax.broadcasted_iota(jnp.int32, (width * BLOCK, q.shape[0]), 0)
            mask = key < (count - first) * BLOCK
            at = [jnp.minimum(a, count - 1) for a in at]
        at = [blocks[1 + a] for a in at]
        k, v = (
            jnp.concatenate([pool[a // FRESH, kv, rows_of(a % FRESH), :] for a in at], axis=0)
            for kv in range(2)
        )
        state = (row[0:1, cols], row[1:2, cols], acc[:, cols])
        state = softmax_step(q, k, v, state, mask)
        row[0:1, cols] = state[0]
        row[1:2, cols] = state[1]
        acc[:, cols] = state[2]

    wide = count // 8

    def eight(n, carry):
        group(n * 8, 8, queries[...].reshape(4 * ROWS, HD), pl.ds(0, 4 * ROWS), False)
        return carry

    lax.fori_loop(0, wide, eight, 0)

    def four(n, carry):
        cols = pl.ds(pl.multiple_of((n % 4) * ROWS, ROWS), ROWS)
        group(wide * 8 + (n // 4) * 4, 4, queries[n % 4], cols, True)
        return carry

    lax.fori_loop(0, (count - wide * 8 + 3) // 4 * 4, four, 0)


STATE = [
    jax.ShapeDtypeStruct((HD, 4 * ROWS), jnp.float32),
    jax.ShapeDtypeStruct((8, 4 * ROWS), jnp.float32),
]


def early_kernel(blocks, fq, g0, g1, y0, z0, acc, row, pool, sems):
    copies = Copies(sems)
    for n, p in enumerate((g0, g1, y0, z0)):
        copies.start(p, pool.at[pl.ds(2 * n, 2)])
    row[0:1, :] = jnp.full((1, 4 * ROWS), -1e30, jnp.float32)
    row[1:2, :] = jnp.zeros((1, 4 * ROWS), jnp.float32)
    acc[...] = jnp.zeros_like(acc)
    copies.wait()
    pool_steps(fq, blocks, pool, acc, row)


def attend_early(blocks, fq, pools):
    return pl.pallas_call(
        early_kernel,
        out_shape=STATE,
        in_specs=[SMEM, VMEM] + [ANY] * 4,
        out_specs=[VMEM] * 2,
        scratch_shapes=[
            pltpu.VMEM((8, 2, ROWS, HD), jnp.bfloat16),
            pltpu.SemaphoreType.DMA((4,)),
        ],
        cost_estimate=pl.CostEstimate(
            flops=4_000_000 * 512, bytes_accessed=4 << 20, transcendentals=4_000_000
        ),
        name="attend_early",
    )(blocks, fq, *pools)


def fresh_kernel(
    blocks, fq, f0, f1, fy, f3, y1, z1, acc, row, acc_out, row_out, fresh, pool, sems
):
    _, _, gi, _ = places()
    copies = [
        pltpu.make_async_copy(f, fresh.at[gi ^ r], sems.at[r])
        for r, f in enumerate((f0, f1, fy.at[0], f3))
    ] + [
        pltpu.make_async_copy(p, pool.at[pl.ds(2 * n, 2)], sems.at[4 + n])
        for n, p in enumerate((y1, z1))
    ]
    for one in copies:
        one.start()
    acc_out[...] = acc[...]
    row_out[...] = row[...]
    for one in copies:
        one.wait()
    for k in range(4):
        n = (4 - k) * ROWS
        cols = pl.ds(k * ROWS, n)
        key = lax.broadcasted_iota(jnp.int32, (ROWS, n), 0)
        query = lax.broadcasted_iota(jnp.int32, (ROWS, n), 1)
        state = (row_out[0:1, cols], row_out[1:2, cols], acc_out[:, cols])
        q = fq[k:].reshape(n, HD)
        state = softmax_step(q, fresh[k, 0], fresh[k, 1], state, key <= query)
        row_out[0:1, cols] = state[0]
        row_out[1:2, cols] = state[1]
        acc_out[:, cols] = state[2]
    pool_steps(fq, blocks, pool, acc_out, row_out)


def attend_fresh(blocks, fq, fresh, pools, acc, row):
    return pl.pallas_call(
        fresh_kernel,
        out_shape=STATE,
        in_specs=[SMEM, VMEM] + [ANY] * 6 + [VMEM] * 2,
        out_specs=[VMEM] * 2,
        scratch_shapes=[
            pltpu.VMEM((4, 2, ROWS, HD), jnp.bfloat16),
            pltpu.VMEM((4, 2, ROWS, HD), jnp.bfloat16),
            pltpu.SemaphoreType.DMA((6,)),
        ],
        cost_estimate=pl.CostEstimate(
            flops=2_600_000 * 512, bytes_accessed=4 << 20, transcendentals=2_600_000
        ),
        name="attend_fresh",
    )(blocks, fq, *fresh, *pools, acc, row)


def late_kernel(
    blocks, fq, d0, d1, acc, row, o0, o1, o2, o3, out1, pool, mixed, rows, sems
):
    _, _, gi, _ = places()
    copies = [
        pltpu.make_async_copy(p, pool.at[pl.ds(2 * n, 2)], sems.at[n])
        for n, p in enumerate((d0, d1))
    ]
    for one in copies:
        one.start()
    for one in copies:
        one.wait()
    mixed[...] = acc[...]
    rows[...] = row[...]
    pool_steps(fq, blocks, pool, mixed, rows)
    mixed[...] = mixed[...] / rows[1:2, :]
    for r, out in enumerate((o0, o1, o2, o3)):
        cols = pl.ds(pl.multiple_of((gi ^ r) * ROWS, ROWS), HALF)
        out[...] = mixed[:, cols].astype(jnp.bfloat16).T
    for k in range(4):
        out1[k] = mixed[:, pl.ds(k * ROWS + HALF, HALF)].astype(jnp.bfloat16).T


def attend_late(blocks, fq, pools, acc, row):
    return pl.pallas_call(
        late_kernel,
        out_shape=[jax.ShapeDtypeStruct((HALF, HD), jnp.bfloat16)] * 4
        + [jax.ShapeDtypeStruct((4, HALF, HD), jnp.bfloat16)],
        in_specs=[SMEM, VMEM] + [ANY] * 2 + [VMEM] * 2,
        out_specs=[VMEM] * 5,
        scratch_shapes=[
            pltpu.VMEM((4, 2, ROWS, HD), jnp.bfloat16),
            pltpu.VMEM((HD, 4 * ROWS), jnp.float32),
            pltpu.VMEM((8, 4 * ROWS), jnp.float32),
            pltpu.SemaphoreType.DMA((2,)),
        ],
        cost_estimate=pl.CostEstimate(
            flops=2_000_000 * 512, bytes_accessed=4 << 20, transcendentals=2_000_000
        ),
        name="attend_late",
    )(blocks, fq, *pools, acc, row)


def project_kernel(far, ordered, a0, ap, am, a2a, a2b, mine, other, out, at, wt, sems):
    core = lax.axis_index("core")
    _, yh, _, head = places()
    head = 2 * yh if ordered else head
    x = lax.axis_index("x")
    half = lax.axis_index("zhi") ^ far
    copies = []

    def copy(source, target):
        one = pltpu.make_async_copy(source, target, sems.at[len(copies)])
        one.start()
        copies.append(one)

    for n in range(4):
        target = wt.at[pl.ds(512 * n, 512)]
        one = pltpu.make_async_copy(mine.at[n], target, sems.at[n])
        two = pltpu.make_async_copy(other.at[n], target, sems.at[n])
        pl.when(half == core)(one.start)
        pl.when(half != core)(two.start)
        copies.append(one)
    for source, step, k0 in ((a0, 0, 0), (ap, 3, 0), (am, 1, 0), (a2a, 2, 0), (a2b, 2, 2)):
        for k in range(source.shape[0]):
            col = ((x + step) % 4) * 512 + (head ^ (k0 + k)) * HD
            copy(source.at[k], at.at[:, pl.ds(pl.multiple_of(col, HD), HD)])
    for one in copies:
        one.wait()

    def tile(n, carry):
        rows = pl.ds(pl.multiple_of(n * 128, 128), 128)
        out[rows, :] = jnp.dot(
            at[rows, :], wt[...], preferred_element_type=jnp.float32
        ).astype(out.dtype)
        return carry

    lax.fori_loop(0, HALF // 128, tile, 0)


def project(far, ordered, dtype, pieces, weights):
    return pl.pallas_call(
        functools.partial(project_kernel, far, ordered),
        out_shape=jax.ShapeDtypeStruct((HALF, COLS), dtype),
        in_specs=[ANY] * 7,
        out_specs=VMEM,
        scratch_shapes=[
            pltpu.VMEM((HALF, 2048), jnp.bfloat16),
            pltpu.VMEM((2048, COLS), jnp.bfloat16),
            pltpu.SemaphoreType.DMA((20,)),
        ],
        cost_estimate=pl.CostEstimate(
            flops=2 * HALF * 2048 * COLS, bytes_accessed=5 << 20, transcendentals=0
        ),
        name=f"project{ordered}_" + ("far" if far else "near"),
    )(*pieces, *weights)


def merge(stats, count):
    mean = sum(s[0] for s in stats) / len(stats)
    square = sum(s[1] + count * jnp.square(s[0] - mean) for s in stats)
    return jnp.stack([mean, square])


def shards(
    queries, new_keys, new_values, pool_keys, pool_values, cache_len, cached_table, free_blocks,
    residual_in, out_weight, out_bias, ln_gain, ln_bias,
):
    after = lambda value, *others: lax.optimization_barrier((value, *others))[0]
    group = ("ylo", "core")
    fq, c0, c1, cy = prep(free_blocks, queries, pool_keys, pool_values)

    fq = lax.all_to_all(fq, group, 0, 0)
    cy = move(cy, ("ylo",))
    g0 = jnp.stack([c0, move(c1, ("core",))])
    y0, z0 = move(g0, ("yhi", "ylo")), move(g0, ("zlo",))
    part, keys_out, values_out, f0, f1, fy, early, mid, late = side(
        after(jnp.zeros((1,), jnp.int32), cy), free_blocks, cached_table, cache_len,
        new_keys, new_values, pool_keys, pool_values, out_weight,
    )

    g1 = after(jnp.stack([cy[0], move(cy[1], ("core",))]), y0, z0)
    y1, z1 = move(g1, ("yhi", "ylo")), move(g1, ("zlo",))
    d0 = move(after(y0, g1), ("zlo",))
    fy = move(after(fy, g1), ("ylo",))
    f1 = move(after(f1, g1), ("core",))
    f3 = move(fy[1], ("core",))

    mine = lax.all_to_all(after(part, g1, fq), "x", 0, 0)

    acc, row = attend_early(early, fq, (g0, g1, y0, z0))
    d1 = move(after(z1, acc), ("yhi", "ylo"))
    acc, row = attend_fresh(mid, fq, (f0, f1, fy, f3), (y1, z1), acc, row)
    *mixed0, mixed1 = attend_late(late, fq, (d0, d1), acc, row)

    sums = []
    for ordered, o in enumerate((mixed0, mixed1)):
        if ordered:
            a0 = lax.all_to_all(o, group, 0, 0)
        else:
            a0 = jnp.stack([o[0]] + [move(o[r], RELATION[r]) for r in (1, 2, 3)])
            other = move(after(mine, a0), ("core",))
        ap, am = move(a0, (), 1), move(a0, (), 3)
        pieces = (a0, ap, am, move(ap[:2], (), 1), move(am[2:], (), 3))
        sent = move(project(1, ordered, jnp.bfloat16, pieces, (mine, other)), ("zhi",))
        near = project(0, ordered, jnp.float32, pieces, (mine, other))
        sums.append(near + sent.astype(jnp.float32))
    stream = (
        residual_in.astype(jnp.float32) + jnp.concatenate(sums, axis=0) + out_bias[None, :]
    )
    mean = jnp.sum(stream, axis=1) / COLS
    square = jnp.sum(jnp.square(stream - mean[:, None]), axis=1)
    stats = jnp.stack([mean, square])
    stats = merge([stats] + [move(stats, (), k) for k in (1, 2, 3)], COLS)
    stats = merge([stats, move(stats, ("zhi",))], 4 * COLS)
    mean, variance = stats[0], stats[1] / D
    normed = (
        (stream - mean[:, None]) * lax.rsqrt(variance[:, None] + 1e-05) * ln_gain[None, :]
        + ln_bias[None, :]
    ).astype(jnp.bfloat16)
    return (stream.astype(jnp.bfloat16), normed, keys_out, values_out)


def solution(mesh):
    fine = Mesh(mesh.devices.reshape(tuple(SIZES.values())), tuple(SIZES))
    both = P(SEQ, HEAD)
    head = P(HEAD)
    in_specs = (both,) * 5 + (P(), P(), P()) + (both, P(HEAD, None), head, head, head)
    return jax.shard_map(
        shards, mesh=fine, in_specs=in_specs, out_specs=(both,) * 4, check_vma=False
    )
```

```python
import functools

import jax
import jax.numpy as jnp
import numpy as np
from jax import lax
from jax.experimental import pallas as pl
from jax.experimental.pallas import tpu as pltpu
from jax.sharding import Mesh
from jax.sharding import PartitionSpec as P

D = 7168
HD = 128
BLOCK = 128
ROWS = 512
HALF = 256
FRESH = 4
COLS = 896
SIZES = {"zlo": 2, "yhi": 2, "ylo": 2, "core": 2, "zhi": 2, "x": 4}
SEQ = ("zlo", "yhi", "ylo", "core")
HEAD = ("zhi", "x")
SCALE2 = HD**-0.5 * 1.4426950408889634
ANY = pl.BlockSpec(memory_space=pl.ANY)
SMEM = pl.BlockSpec(memory_space=pltpu.SMEM)
VMEM = pl.BlockSpec(memory_space=pltpu.VMEM)


def move(value, flips=(), x_step=0):
    axes = tuple(flips) + (("x",) if x_step else ())
    sizes = [SIZES[a] for a in axes]
    pairs = []
    for source in range(int(np.prod(sizes))):
        place = list(np.unravel_index(source, sizes))
        for k, a in enumerate(axes):
            place[k] = (place[k] + x_step) % 4 if a == "x" else 1 - place[k]
        pairs.append((source, int(np.ravel_multi_index(place, sizes))))
    return lax.ppermute(value, axes, pairs)


RELATION = ((), ("core",), ("ylo",), ("ylo", "core"))


def places():
    z, yh, yl, c = (lax.axis_index(a) for a in SEQ)
    group_index = yl * 2 + c
    head = (yl ^ yh) * 2 + c
    return z, yh, group_index, head


def find_spare(free, spare):
    z, yh, gi, _ = places()
    prompt = z * 2 + yh
    count = jnp.int32(0)
    for lb in range(8):
        block = (prompt * 4 + gi) * 8 + lb
        taken = free[prompt, gi * FRESH] == block
        for k in range(1, FRESH):
            taken = taken | (free[prompt, gi * FRESH + k] == block)

        @pl.when(jnp.logical_not(taken) & (count < FRESH))
        def _():
            spare[count] = lb

        count = count + jnp.where(taken, 0, 1)


class Copies:
    def __init__(self, sems):
        self.sems, self.open, self.used = sems, [], 0

    def start(self, source, target):
        one = pltpu.make_async_copy(source, target, self.sems.at[self.used])
        self.used += 1
        one.start()
        self.open.append(one)
        return one

    def wait(self):
        for one in self.open:
            one.wait()
        self.open = []


def rows_of(block):
    return pl.ds(pl.multiple_of(block * BLOCK, BLOCK), BLOCK)


def cols_of(head):
    return pl.ds(pl.multiple_of(head * HD, HD), HD)


def prep_kernel(free, q, pk, pv, fq, c0, c1, cy, spare, held, held_q, sems):
    _, yh, _, head = places()
    copies = Copies(sems)
    query = pltpu.make_async_copy(q, held_q, sems.at[sems.shape[0] - 1])
    query.start()
    find_spare(free, spare)
    for s in range(FRESH):
        for kv, source in enumerate((pk, pv)):
            copies.start(source.at[rows_of(spare[s])], held.at[kv, pl.ds(s * BLOCK, BLOCK)])
    copies.wait()
    for r, out in ((1, c1), (2, cy.at[0]), (3, cy.at[1]), (0, c0)):
        for kv in range(2):
            copies.start(held.at[kv, :, cols_of(head ^ r)], out.at[kv])
    query.wait()
    for k in range(4):
        copies.start(held_q.at[:, cols_of(k ^ (2 * yh))], fq.at[k])
    copies.wait()


def prep(free, q, pk, pv):
    shape = lambda *s: jax.ShapeDtypeStruct(s, jnp.bfloat16)
    return pl.pallas_call(
        prep_kernel,
        out_shape=[shape(4, ROWS, HD)] + [shape(2, ROWS, HD)] * 2 + [shape(2, 2, ROWS, HD)],
        in_specs=[SMEM] + [ANY] * 3,
        out_specs=[ANY] * 4,
        scratch_shapes=[
            pltpu.SMEM((FRESH,), jnp.int32),
            pltpu.VMEM((2, ROWS, 512), jnp.bfloat16),
            pltpu.VMEM((ROWS, 512), jnp.bfloat16),
            pltpu.SemaphoreType.DMA((24,)),
        ],
        cost_estimate=pl.CostEstimate(flops=0, bytes_accessed=4 << 20, transcendentals=0),
        name="prep",
    )(free, q, pk, pv)


def side_kernel(
    gate, free, table, length, nk, nv, pk, pv, weight,
    cut, ko, vo, f0, f1, fy, early, mid, late, spare, wide, new, old, sems,
):
    z, yh, gi, head = places()
    core = lax.axis_index("core")
    prompt = z * 2 + yh
    copies = Copies(sems)
    reads = [
        copies.start(weight.at[:, pl.ds(pl.multiple_of((core * 4 + n) * COLS, HD), COLS)], wide.at[n])
        for n in range(4)
    ]
    for kv, source in enumerate((nk, nv)):
        copies.start(source, new.at[kv])
    find_spare(free, spare)
    for s in range(FRESH):
        for kv, source in enumerate((pk, pv)):
            copies.start(source.at[rows_of(spare[s])], old.at[kv, pl.ds(s * BLOCK, BLOCK)])

    def one(n, counts):
        block = jnp.clip(table[prompt, n], 0, 127)
        owner, place = block // 32, (block // 8) % 4
        rank = block % 8
        for k in range(FRESH):
            rank = rank - jnp.where(free[owner, place * FRESH + k] < block, 1, 0)
        rank = jnp.clip(rank, 0, FRESH - 1)
        far_y = (owner % 2) ^ yh
        group = ((owner // 2) ^ z) * 2 + far_y
        r = place ^ gi ^ (2 * far_y)
        is_late = jnp.where(group == 3, 1, 0)
        is_mid = jnp.where((group > 0) & (group < 3) & (r > 1), 1, 0)
        early[1 + counts[0]] = (
            jnp.clip(jnp.where(group == 0, r, 2 + 2 * group + r), 0, 7) * FRESH + rank
        )
        mid[1 + counts[1]] = jnp.clip(2 * group + r - 4, 0, 3) * FRESH + rank
        late[1 + counts[2]] = r * FRESH + rank
        return counts[0] + 1 - is_late - is_mid, counts[1] + is_mid, counts[2] + is_late

    counts = lax.fori_loop(0, length[prompt] // BLOCK, one, (jnp.int32(0),) * 3)
    for listed, count in zip((early, mid, late), counts):
        listed[0] = count
    copies.wait()
    for n in range(4):
        copies.start(wide.at[n], cut.at[n])
    for kv, out in enumerate((ko, vo)):
        for r, target in ((2, fy.at[0]), (3, fy.at[1]), (1, f1), (0, f0)):
            copies.start(new.at[kv, :, cols_of(head ^ r)], target.at[kv])
        for s in range(FRESH):
            rows = pl.ds(s * BLOCK, BLOCK)
            into = jnp.clip(free[prompt, gi * FRESH + s] - (prompt * 4 + gi) * 8, 0, 7)
            copies.start(new.at[kv, rows], out.at[rows_of(into)])
            copies.start(old.at[kv, rows], out.at[rows_of(spare[s])])
    copies.wait()


def side(gate, free, table, length, nk, nv, pk, pv, weight):
    shape = lambda *s: jax.ShapeDtypeStruct(s, jnp.bfloat16)
    return pl.pallas_call(
        side_kernel,
        out_shape=[shape(4, 512, COLS)]
        + [shape(1024, 512)] * 2
        + [shape(2, ROWS, HD)] * 2
        + [shape(2, 2, ROWS, HD)]
        + [jax.ShapeDtypeStruct((40,), jnp.int32)] * 3,
        in_specs=[SMEM] * 4 + [ANY] * 5,
        out_specs=[ANY] * 6 + [SMEM] * 3,
        scratch_shapes=[
            pltpu.SMEM((FRESH,), jnp.int32),
            pltpu.VMEM((4, 512, COLS), jnp.bfloat16),
            pltpu.VMEM((2, ROWS, 512), jnp.bfloat16),
            pltpu.VMEM((2, ROWS, 512), jnp.bfloat16),
            pltpu.SemaphoreType.DMA((48,)),
        ],
        cost_estimate=pl.CostEstimate(flops=0, bytes_accessed=14 << 20, transcendentals=0),
        name="side",
    )(gate, free, table, length, nk, nv, pk, pv, weight)


def softmax_step(q, k, v, state, mask=None):
    peak, total, acc = state
    s = lax.dot_general(k, q, (((1,), (1,)), ((), ())), preferred_element_type=jnp.float32)
    if mask is not None:
        width = mask.shape[1]
        parts = [jnp.where(mask, s[:, :width], -1e30)]
        if width < s.shape[1]:
            parts.append(s[:, width:])
        s = jnp.concatenate(parts, axis=1)
    new_peak = jnp.maximum(peak, jnp.max(s, axis=0, keepdims=True))
    p = jnp.exp2((s - new_peak) * SCALE2)
    fade = jnp.exp2((peak - new_peak) * SCALE2)
    total = total * fade + jnp.sum(p, axis=0, keepdims=True)
    acc = acc * fade + lax.dot_general(
        v, p.astype(jnp.bfloat16), (((0,), (0,)), ((), ())), preferred_element_type=jnp.float32
    )
    return new_peak, total, acc


def pool_steps(queries, blocks, pool, acc, row):
    count = blocks[0]

    def group(first, width, q, cols, masked):
        at = [first + m for m in range(width)]
        mask = None
        if masked:
            key = lax.broadcasted_iota(jnp.int32, (width * BLOCK, q.shape[0]), 0)
            mask = key < (count - first) * BLOCK
            at = [jnp.minimum(a, count - 1) for a in at]
        at = [blocks[1 + a] for a in at]
        k, v = (
            jnp.concatenate([pool[a // FRESH, kv, rows_of(a % FRESH), :] for a in at], axis=0)
            for kv in range(2)
        )
        state = (row[0:1, cols], row[1:2, cols], acc[:, cols])
        state = softmax_step(q, k, v, state, mask)
        row[0:1, cols] = state[0]
        row[1:2, cols] = state[1]
        acc[:, cols] = state[2]

    wide = count // 8

    def eight(n, carry):
        group(n * 8, 8, queries[...].reshape(4 * ROWS, HD), pl.ds(0, 4 * ROWS), False)
        return carry

    lax.fori_loop(0, wide, eight, 0)

    def four(n, carry):
        cols = pl.ds(pl.multiple_of((n % 4) * ROWS, ROWS), ROWS)
        group(wide * 8 + (n // 4) * 4, 4, queries[n % 4], cols, True)
        return carry

    lax.fori_loop(0, (count - wide * 8 + 3) // 4 * 4, four, 0)


STATE = [
    jax.ShapeDtypeStruct((HD, 4 * ROWS), jnp.float32),
    jax.ShapeDtypeStruct((8, 4 * ROWS), jnp.float32),
]


def early_kernel(blocks, fq, g0, g1, y0, z0, acc, row, pool, sems):
    copies = Copies(sems)
    for n, p in enumerate((g0, g1, y0, z0)):
        copies.start(p, pool.at[pl.ds(2 * n, 2)])
    row[0:1, :] = jnp.full((1, 4 * ROWS), -1e30, jnp.float32)
    row[1:2, :] = jnp.zeros((1, 4 * ROWS), jnp.float32)
    acc[...] = jnp.zeros_like(acc)
    copies.wait()
    pool_steps(fq, blocks, pool, acc, row)


def attend_early(blocks, fq, pools):
    return pl.pallas_call(
        early_kernel,
        out_shape=STATE,
        in_specs=[SMEM, VMEM] + [ANY] * 4,
        out_specs=[VMEM] * 2,
        scratch_shapes=[
            pltpu.VMEM((8, 2, ROWS, HD), jnp.bfloat16),
            pltpu.SemaphoreType.DMA((4,)),
        ],
        cost_estimate=pl.CostEstimate(
            flops=4_000_000 * 512, bytes_accessed=4 << 20, transcendentals=4_000_000
        ),
        name="attend_early",
    )(blocks, fq, *pools)


def fresh_kernel(
    blocks, fq, f0, f1, fy, f3, y1, z1, acc, row, acc_out, row_out, fresh, pool, sems
):
    _, _, gi, _ = places()
    copies = [
        pltpu.make_async_copy(f, fresh.at[gi ^ r], sems.at[r])
        for r, f in enumerate((f0, f1, fy.at[0], f3))
    ] + [
        pltpu.make_async_copy(p, pool.at[pl.ds(2 * n, 2)], sems.at[4 + n])
        for n, p in enumerate((y1, z1))
    ]
    for one in copies:
        one.start()
    acc_out[...] = acc[...]
    row_out[...] = row[...]
    for one in copies:
        one.wait()
    for k in range(4):
        n = (4 - k) * ROWS
        cols = pl.ds(k * ROWS, n)
        key = lax.broadcasted_iota(jnp.int32, (ROWS, ROWS), 0)
        query = lax.broadcasted_iota(jnp.int32, (ROWS, ROWS), 1)
        state = (row_out[0:1, cols], row_out[1:2, cols], acc_out[:, cols])
        q = fq[k:].reshape(n, HD)
        state = softmax_step(q, fresh[k, 0], fresh[k, 1], state, key <= query)
        row_out[0:1, cols] = state[0]
        row_out[1:2, cols] = state[1]
        acc_out[:, cols] = state[2]
    pool_steps(fq, blocks, pool, acc_out, row_out)


def attend_fresh(blocks, fq, fresh, pools, acc, row):
    return pl.pallas_call(
        fresh_kernel,
        out_shape=STATE,
        in_specs=[SMEM, VMEM] + [ANY] * 6 + [VMEM] * 2,
        out_specs=[VMEM] * 2,
        scratch_shapes=[
            pltpu.VMEM((4, 2, ROWS, HD), jnp.bfloat16),
            pltpu.VMEM((4, 2, ROWS, HD), jnp.bfloat16),
            pltpu.SemaphoreType.DMA((6,)),
        ],
        cost_estimate=pl.CostEstimate(
            flops=2_600_000 * 512, bytes_accessed=4 << 20, transcendentals=2_600_000
        ),
        name="attend_fresh",
    )(blocks, fq, *fresh, *pools, acc, row)


def late_kernel(
    blocks, fq, d0, d1, acc, row, o0, o1, o2, o3, out1, pool, mixed, rows, sems
):
    _, _, gi, _ = places()
    copies = [
        pltpu.make_async_copy(p, pool.at[pl.ds(2 * n, 2)], sems.at[n])
        for n, p in enumerate((d0, d1))
    ]
    for one in copies:
        one.start()
    for one in copies:
        one.wait()
    mixed[...] = acc[...]
    rows[...] = row[...]
    pool_steps(fq, blocks, pool, mixed, rows)
    mixed[...] = mixed[...] / rows[1:2, :]
    for r, out in enumerate((o0, o1, o2, o3)):
        cols = pl.ds(pl.multiple_of((gi ^ r) * ROWS, ROWS), HALF)
        out[...] = mixed[:, cols].astype(jnp.bfloat16).T
    for k in range(4):
        out1[k] = mixed[:, pl.ds(k * ROWS + HALF, HALF)].astype(jnp.bfloat16).T


def attend_late(blocks, fq, pools, acc, row):
    return pl.pallas_call(
        late_kernel,
        out_shape=[jax.ShapeDtypeStruct((HALF, HD), jnp.bfloat16)] * 4
        + [jax.ShapeDtypeStruct((4, HALF, HD), jnp.bfloat16)],
        in_specs=[SMEM, VMEM] + [ANY] * 2 + [VMEM] * 2,
        out_specs=[VMEM] * 5,
        scratch_shapes=[
            pltpu.VMEM((4, 2, ROWS, HD), jnp.bfloat16),
            pltpu.VMEM((HD, 4 * ROWS), jnp.float32),
            pltpu.VMEM((8, 4 * ROWS), jnp.float32),
            pltpu.SemaphoreType.DMA((2,)),
        ],
        cost_estimate=pl.CostEstimate(
            flops=2_000_000 * 512, bytes_accessed=4 << 20, transcendentals=2_000_000
        ),
        name="attend_late",
    )(blocks, fq, *pools, acc, row)


def project_kernel(far, ordered, a0, ap, am, a2a, a2b, mine, other, out, at, wt, sems):
    core = lax.axis_index("core")
    _, yh, _, head = places()
    head = 2 * yh if ordered else head
    x = lax.axis_index("x")
    half = lax.axis_index("zhi") ^ far
    copies = Copies(sems)
    for source, step, k0 in ((a0, 0, 0), (ap, 3, 0), (am, 1, 0), (a2a, 2, 0), (a2b, 2, 2)):
        for k in range(source.shape[0]):
            col = ((x + step) % 4) * 512 + (head ^ (k0 + k)) * HD
            copies.start(source.at[k], at.at[:, pl.ds(pl.multiple_of(col, HD), HD)])
    parts = (slice(0, 512), slice(512, COLS))
    loads = []
    for m, part in enumerate(parts):
        for n in range(4):
            target = wt.at[pl.ds(512 * n, 512), part]
            sem = sems.at[copies.used + 4 * m + n]
            one = pltpu.make_async_copy(mine.at[n, :, part], target, sem)
            two = pltpu.make_async_copy(other.at[n, :, part], target, sem)
            pl.when(half == core)(one.start)
            pl.when(half != core)(two.start)
            loads.append(one)
    copies.wait()
    for m, part in enumerate(parts):
        for one in loads[4 * m : 4 * m + 4]:
            one.wait()

        def tile(n, carry):
            rows = pl.ds(pl.multiple_of(n * 128, 128), 128)
            out[rows, part] = jnp.dot(
                at[rows, :], wt[:, part], preferred_element_type=jnp.float32
            ).astype(out.dtype)
            return carry

        lax.fori_loop(0, HALF // 128, tile, 0)


def project(far, ordered, dtype, pieces, weights):
    return pl.pallas_call(
        functools.partial(project_kernel, far, ordered),
        out_shape=jax.ShapeDtypeStruct((HALF, COLS), dtype),
        in_specs=[ANY] * 7,
        out_specs=VMEM,
        scratch_shapes=[
            pltpu.VMEM((HALF, 2048), jnp.bfloat16),
            pltpu.VMEM((2048, COLS), jnp.bfloat16),
            pltpu.SemaphoreType.DMA((24,)),
        ],
        cost_estimate=pl.CostEstimate(
            flops=2 * HALF * 2048 * COLS, bytes_accessed=5 << 20, transcendentals=0
        ),
        name=f"project{ordered}_" + ("far" if far else "near"),
    )(*pieces, *weights)


def merge(stats, count):
    mean = sum(s[0] for s in stats) / len(stats)
    square = sum(s[1] + count * jnp.square(s[0] - mean) for s in stats)
    return jnp.stack([mean, square])


def shards(
    queries, new_keys, new_values, pool_keys, pool_values, cache_len, cached_table, free_blocks,
    residual_in, out_weight, out_bias, ln_gain, ln_bias,
):
    after = lambda value, *others: lax.optimization_barrier((value, *others))[0]
    group = ("ylo", "core")
    fq, c0, c1, cy = prep(free_blocks, queries, pool_keys, pool_values)

    fq = lax.all_to_all(fq, group, 0, 0)
    cy = move(cy, ("ylo",))
    g0 = jnp.stack([c0, move(c1, ("core",))])
    y0, z0 = move(g0, ("yhi", "ylo")), move(g0, ("zlo",))
    part, keys_out, values_out, f0, f1, fy, early, mid, late = side(
        after(jnp.zeros((1,), jnp.int32), cy), free_blocks, cached_table, cache_len,
        new_keys, new_values, pool_keys, pool_values, out_weight,
    )

    g1 = after(jnp.stack([cy[0], move(cy[1], ("core",))]), y0, z0)
    y1, z1 = move(g1, ("yhi", "ylo")), move(g1, ("zlo",))
    d0 = move(after(y0, g1), ("zlo",))
    fy = move(after(fy, g1), ("ylo",))
    f1 = move(after(f1, g1), ("core",))
    f3 = move(fy[1], ("core",))

    mine = lax.all_to_all(after(part, g1, fq), "x", 0, 0)

    acc, row = attend_early(early, fq, (g0, g1, y0, z0))
    d1 = move(after(z1, acc), ("yhi", "ylo"))
    acc, row = attend_fresh(mid, fq, (f0, f1, fy, f3), (y1, z1), acc, row)
    *mixed0, mixed1 = attend_late(late, fq, (d0, d1), acc, row)

    sums = []
    for ordered, o in enumerate((mixed0, mixed1)):
        if ordered:
            a0 = lax.all_to_all(o, group, 0, 0)
        else:
            a0 = jnp.stack([o[0]] + [move(o[r], RELATION[r]) for r in (1, 2, 3)])
            other = move(after(mine, a0), ("core",))
        ap, am = move(a0, (), 1), move(a0, (), 3)
        pieces = (a0, ap, am, move(ap[:2], (), 1), move(am[2:], (), 3))
        sent = move(project(1, ordered, jnp.bfloat16, pieces, (mine, other)), ("zhi",))
        near = project(0, ordered, jnp.float32, pieces, (mine, other))
        sums.append(near + sent.astype(jnp.float32))
    stream = (
        residual_in.astype(jnp.float32) + jnp.concatenate(sums, axis=0) + out_bias[None, :]
    )
    mean = jnp.sum(stream, axis=1) / COLS
    square = jnp.sum(jnp.square(stream - mean[:, None]), axis=1)
    stats = jnp.stack([mean, square])
    stats = merge([stats] + [move(stats, (), k) for k in (1, 2, 3)], COLS)
    stats = merge([stats, move(stats, ("zhi",))], 4 * COLS)
    mean, variance = stats[0], stats[1] / D
    normed = (
        (stream - mean[:, None]) * lax.rsqrt(variance[:, None] + 1e-05) * ln_gain[None, :]
        + ln_bias[None, :]
    ).astype(jnp.bfloat16)
    return (stream.astype(jnp.bfloat16), normed, keys_out, values_out)


def solution(mesh):
    fine = Mesh(mesh.devices.reshape(tuple(SIZES.values())), tuple(SIZES))
    both = P(SEQ, HEAD)
    head = P(HEAD)
    in_specs = (both,) * 5 + (P(), P(), P()) + (both, P(HEAD, None), head, head, head)
    return jax.shard_map(
        shards, mesh=fine, in_specs=in_specs, out_specs=(both,) * 4, check_vma=False
    )
```

```python
import functools

import jax
import jax.numpy as jnp
import numpy as np
from jax import lax
from jax.experimental import pallas as pl
from jax.experimental.pallas import tpu as pltpu
from jax.sharding import Mesh
from jax.sharding import PartitionSpec as P

D = 7168
HD = 128
BLOCK = 128
ROWS = 512
HALF = 256
FRESH = 4
COLS = 896
SIZES = {"zlo": 2, "yhi": 2, "ylo": 2, "core": 2, "zhi": 2, "x": 4}
SEQ = ("zlo", "yhi", "ylo", "core")
HEAD = ("zhi", "x")
SCALE2 = HD**-0.5 * 1.4426950408889634
ANY = pl.BlockSpec(memory_space=pl.ANY)
SMEM = pl.BlockSpec(memory_space=pltpu.SMEM)
VMEM = pl.BlockSpec(memory_space=pltpu.VMEM)


def move(value, flips=(), x_step=0):
    axes = tuple(flips) + (("x",) if x_step else ())
    sizes = [SIZES[a] for a in axes]
    pairs = []
    for source in range(int(np.prod(sizes))):
        place = list(np.unravel_index(source, sizes))
        for k, a in enumerate(axes):
            place[k] = (place[k] + x_step) % 4 if a == "x" else 1 - place[k]
        pairs.append((source, int(np.ravel_multi_index(place, sizes))))
    return lax.ppermute(value, axes, pairs)


RELATION = ((), ("core",), ("ylo",), ("ylo", "core"))


def places():
    z, yh, yl, c = (lax.axis_index(a) for a in SEQ)
    group_index = yl * 2 + c
    head = (yl ^ yh) * 2 + c
    return z, yh, group_index, head


def find_spare(free, spare):
    z, yh, gi, _ = places()
    prompt = z * 2 + yh
    count = jnp.int32(0)
    for lb in range(8):
        block = (prompt * 4 + gi) * 8 + lb
        taken = free[prompt, gi * FRESH] == block
        for k in range(1, FRESH):
            taken = taken | (free[prompt, gi * FRESH + k] == block)

        @pl.when(jnp.logical_not(taken) & (count < FRESH))
        def _():
            spare[count] = lb

        count = count + jnp.where(taken, 0, 1)


class Copies:
    def __init__(self, sems):
        self.sems, self.open, self.used = sems, [], 0

    def start(self, source, target):
        one = pltpu.make_async_copy(source, target, self.sems.at[self.used])
        self.used += 1
        one.start()
        self.open.append(one)
        return one

    def wait(self):
        for one in self.open:
            one.wait()
        self.open = []


def rows_of(block):
    return pl.ds(pl.multiple_of(block * BLOCK, BLOCK), BLOCK)


def cols_of(head):
    return pl.ds(pl.multiple_of(head * HD, HD), HD)


def prep_kernel(free, q, pk, pv, fq, c0, c1, cy, spare, held, held_q, sems):
    _, yh, _, head = places()
    copies = Copies(sems)
    query = pltpu.make_async_copy(q, held_q, sems.at[sems.shape[0] - 1])
    query.start()
    find_spare(free, spare)
    for s in range(FRESH):
        for kv, source in enumerate((pk, pv)):
            copies.start(source.at[rows_of(spare[s])], held.at[kv, pl.ds(s * BLOCK, BLOCK)])
    copies.wait()
    for r, out in ((1, c1), (2, cy.at[0]), (3, cy.at[1]), (0, c0)):
        for kv in range(2):
            copies.start(held.at[kv, :, cols_of(head ^ r)], out.at[kv])
    query.wait()
    for k in range(4):
        copies.start(held_q.at[:, cols_of(k ^ (2 * yh))], fq.at[k])
    copies.wait()


def prep(free, q, pk, pv):
    shape = lambda *s: jax.ShapeDtypeStruct(s, jnp.bfloat16)
    return pl.pallas_call(
        prep_kernel,
        out_shape=[shape(4, ROWS, HD)] + [shape(2, ROWS, HD)] * 2 + [shape(2, 2, ROWS, HD)],
        in_specs=[SMEM] + [ANY] * 3,
        out_specs=[ANY] * 4,
        scratch_shapes=[
            pltpu.SMEM((FRESH,), jnp.int32),
            pltpu.VMEM((2, ROWS, 512), jnp.bfloat16),
            pltpu.VMEM((ROWS, 512), jnp.bfloat16),
            pltpu.SemaphoreType.DMA((24,)),
        ],
        cost_estimate=pl.CostEstimate(flops=0, bytes_accessed=4 << 20, transcendentals=0),
        name="prep",
    )(free, q, pk, pv)


def side_kernel(
    gate, free, table, length, nk, nv, pk, pv, weight,
    cut, ko, vo, f0, f1, fy, early, mid, late, spare, wide, new, old, sems,
):
    z, yh, gi, head = places()
    core = lax.axis_index("core")
    prompt = z * 2 + yh
    copies = Copies(sems)
    reads = [
        copies.start(weight.at[:, pl.ds(pl.multiple_of((core * 4 + n) * COLS, HD), COLS)], wide.at[n])
        for n in range(4)
    ]
    for kv, source in enumerate((nk, nv)):
        copies.start(source, new.at[kv])
    find_spare(free, spare)
    for s in range(FRESH):
        for kv, source in enumerate((pk, pv)):
            copies.start(source.at[rows_of(spare[s])], old.at[kv, pl.ds(s * BLOCK, BLOCK)])

    def one(n, counts):
        block = jnp.clip(table[prompt, n], 0, 127)
        owner, place = block // 32, (block // 8) % 4
        rank = block % 8
        for k in range(FRESH):
            rank = rank - jnp.where(free[owner, place * FRESH + k] < block, 1, 0)
        rank = jnp.clip(rank, 0, FRESH - 1)
        far_y = (owner % 2) ^ yh
        group = ((owner // 2) ^ z) * 2 + far_y
        r = place ^ gi ^ (2 * far_y)
        is_late = jnp.where(group == 3, 1, 0)
        is_mid = jnp.where((group > 0) & (group < 3) & (r > 1), 1, 0)
        early[1 + counts[0]] = (
            jnp.clip(jnp.where(group == 0, r, 2 + 2 * group + r), 0, 7) * FRESH + rank
        )
        mid[1 + counts[1]] = jnp.clip(2 * group + r - 4, 0, 3) * FRESH + rank
        late[1 + counts[2]] = r * FRESH + rank
        return counts[0] + 1 - is_late - is_mid, counts[1] + is_mid, counts[2] + is_late

    counts = lax.fori_loop(0, length[prompt] // BLOCK, one, (jnp.int32(0),) * 3)
    for listed, count in zip((early, mid, late), counts):
        listed[0] = count
    copies.wait()
    for n in range(4):
        copies.start(wide.at[n], cut.at[n])
    for kv, out in enumerate((ko, vo)):
        for r, target in ((2, fy.at[0]), (3, fy.at[1]), (1, f1), (0, f0)):
            copies.start(new.at[kv, :, cols_of(head ^ r)], target.at[kv])
        for s in range(FRESH):
            rows = pl.ds(s * BLOCK, BLOCK)
            into = jnp.clip(free[prompt, gi * FRESH + s] - (prompt * 4 + gi) * 8, 0, 7)
            copies.start(new.at[kv, rows], out.at[rows_of(into)])
            copies.start(old.at[kv, rows], out.at[rows_of(spare[s])])
    copies.wait()


def side(gate, free, table, length, nk, nv, pk, pv, weight):
    shape = lambda *s: jax.ShapeDtypeStruct(s, jnp.bfloat16)
    return pl.pallas_call(
        side_kernel,
        out_shape=[shape(4, 512, COLS)]
        + [shape(1024, 512)] * 2
        + [shape(2, ROWS, HD)] * 2
        + [shape(2, 2, ROWS, HD)]
        + [jax.ShapeDtypeStruct((40,), jnp.int32)] * 3,
        in_specs=[SMEM] * 4 + [ANY] * 5,
        out_specs=[ANY] * 6 + [SMEM] * 3,
        scratch_shapes=[
            pltpu.SMEM((FRESH,), jnp.int32),
            pltpu.VMEM((4, 512, COLS), jnp.bfloat16),
            pltpu.VMEM((2, ROWS, 512), jnp.bfloat16),
            pltpu.VMEM((2, ROWS, 512), jnp.bfloat16),
            pltpu.SemaphoreType.DMA((48,)),
        ],
        cost_estimate=pl.CostEstimate(flops=0, bytes_accessed=14 << 20, transcendentals=0),
        name="side",
    )(gate, free, table, length, nk, nv, pk, pv, weight)


def softmax_step(q, k, v, state, mask=None):
    peak, total, acc = state
    s = lax.dot_general(k, q, (((1,), (1,)), ((), ())), preferred_element_type=jnp.float32)
    if mask is not None:
        width = mask.shape[1]
        parts = [jnp.where(mask, s[:, :width], -1e30)]
        if width < s.shape[1]:
            parts.append(s[:, width:])
        s = jnp.concatenate(parts, axis=1)
    new_peak = jnp.maximum(peak, jnp.max(s, axis=0, keepdims=True))
    p = jnp.exp2((s - new_peak) * SCALE2)
    fade = jnp.exp2((peak - new_peak) * SCALE2)
    total = total * fade + jnp.sum(p, axis=0, keepdims=True)
    acc = acc * fade + lax.dot_general(
        v, p.astype(jnp.bfloat16), (((0,), (0,)), ((), ())), preferred_element_type=jnp.float32
    )
    return new_peak, total, acc


def pool_steps(queries, blocks, pool, acc, row):
    count = blocks[0]

    def group(first, width, q, cols, masked):
        at = [first + m for m in range(width)]
        mask = None
        if masked:
            key = lax.broadcasted_iota(jnp.int32, (width * BLOCK, q.shape[0]), 0)
            mask = key < (count - first) * BLOCK
            at = [jnp.minimum(a, count - 1) for a in at]
        at = [blocks[1 + a] for a in at]
        k, v = (
            jnp.concatenate([pool[a // FRESH, kv, rows_of(a % FRESH), :] for a in at], axis=0)
            for kv in range(2)
        )
        state = (row[0:1, cols], row[1:2, cols], acc[:, cols])
        state = softmax_step(q, k, v, state, mask)
        row[0:1, cols] = state[0]
        row[1:2, cols] = state[1]
        acc[:, cols] = state[2]

    wide = count // 8

    def eight(n, carry):
        group(n * 8, 8, queries[...].reshape(4 * ROWS, HD), pl.ds(0, 4 * ROWS), False)
        return carry

    lax.fori_loop(0, wide, eight, 0)

    def four(n, carry):
        cols = pl.ds(pl.multiple_of((n % 4) * ROWS, ROWS), ROWS)
        group(wide * 8 + (n // 4) * 4, 4, queries[n % 4], cols, True)
        return carry

    lax.fori_loop(0, (count - wide * 8 + 3) // 4 * 4, four, 0)


STATE = [
    jax.ShapeDtypeStruct((HD, 4 * ROWS), jnp.float32),
    jax.ShapeDtypeStruct((8, 4 * ROWS), jnp.float32),
]


def early_kernel(blocks, fq, g0, g1, y0, z0, acc, row, pool, sems):
    copies = Copies(sems)
    for n, p in enumerate((g0, g1, y0, z0)):
        copies.start(p, pool.at[pl.ds(2 * n, 2)])
    row[0:1, :] = jnp.full((1, 4 * ROWS), -1e30, jnp.float32)
    row[1:2, :] = jnp.zeros((1, 4 * ROWS), jnp.float32)
    acc[...] = jnp.zeros_like(acc)
    copies.wait()
    pool_steps(fq, blocks, pool, acc, row)


def attend_early(blocks, fq, pools):
    return pl.pallas_call(
        early_kernel,
        out_shape=STATE,
        in_specs=[SMEM, VMEM] + [ANY] * 4,
        out_specs=[VMEM] * 2,
        scratch_shapes=[
            pltpu.VMEM((8, 2, ROWS, HD), jnp.bfloat16),
            pltpu.SemaphoreType.DMA((4,)),
        ],
        cost_estimate=pl.CostEstimate(
            flops=4_000_000 * 512, bytes_accessed=4 << 20, transcendentals=4_000_000
        ),
        name="attend_early",
    )(blocks, fq, *pools)


def fresh_kernel(
    blocks, fq, f0, f1, fy, f3, y1, z1, acc, row, acc_out, row_out, fresh, pool, sems
):
    _, _, gi, _ = places()
    copies = [
        pltpu.make_async_copy(f, fresh.at[gi ^ r], sems.at[r])
        for r, f in enumerate((f0, f1, fy.at[0], f3))
    ] + [
        pltpu.make_async_copy(p, pool.at[pl.ds(2 * n, 2)], sems.at[4 + n])
        for n, p in enumerate((y1, z1))
    ]
    for one in copies:
        one.start()
    acc_out[...] = acc[...]
    row_out[...] = row[...]
    for one in copies:
        one.wait()
    for k in range(4):
        n = (4 - k) * ROWS
        cols = pl.ds(k * ROWS, n)
        key = lax.broadcasted_iota(jnp.int32, (ROWS, ROWS), 0)
        query = lax.broadcasted_iota(jnp.int32, (ROWS, ROWS), 1)
        state = (row_out[0:1, cols], row_out[1:2, cols], acc_out[:, cols])
        q = fq[k:].reshape(n, HD)
        state = softmax_step(q, fresh[k, 0], fresh[k, 1], state, key <= query)
        row_out[0:1, cols] = state[0]
        row_out[1:2, cols] = state[1]
        acc_out[:, cols] = state[2]
    pool_steps(fq, blocks, pool, acc_out, row_out)


def attend_fresh(blocks, fq, fresh, pools, acc, row):
    return pl.pallas_call(
        fresh_kernel,
        out_shape=STATE,
        in_specs=[SMEM, VMEM] + [ANY] * 6 + [VMEM] * 2,
        out_specs=[VMEM] * 2,
        scratch_shapes=[
            pltpu.VMEM((4, 2, ROWS, HD), jnp.bfloat16),
            pltpu.VMEM((4, 2, ROWS, HD), jnp.bfloat16),
            pltpu.SemaphoreType.DMA((6,)),
        ],
        cost_estimate=pl.CostEstimate(
            flops=2_600_000 * 512, bytes_accessed=4 << 20, transcendentals=2_600_000
        ),
        name="attend_fresh",
        compiler_params=pltpu.CompilerParams(vmem_limit_bytes=67_043_328),
    )(blocks, fq, *fresh, *pools, acc, row)


def late_kernel(
    blocks, fq, d0, d1, acc, row, o0, o1, o2, o3, out1, pool, mixed, rows, sems
):
    _, _, gi, _ = places()
    copies = [
        pltpu.make_async_copy(p, pool.at[pl.ds(2 * n, 2)], sems.at[n])
        for n, p in enumerate((d0, d1))
    ]
    for one in copies:
        one.start()
    for one in copies:
        one.wait()
    mixed[...] = acc[...]
    rows[...] = row[...]
    pool_steps(fq, blocks, pool, mixed, rows)
    mixed[...] = mixed[...] / rows[1:2, :]
    for r, out in enumerate((o0, o1, o2, o3)):
        cols = pl.ds(pl.multiple_of((gi ^ r) * ROWS, ROWS), HALF)
        out[...] = mixed[:, cols].astype(jnp.bfloat16).T
    for k in range(4):
        out1[k] = mixed[:, pl.ds(k * ROWS + HALF, HALF)].astype(jnp.bfloat16).T


def attend_late(blocks, fq, pools, acc, row):
    return pl.pallas_call(
        late_kernel,
        out_shape=[jax.ShapeDtypeStruct((HALF, HD), jnp.bfloat16)] * 4
        + [jax.ShapeDtypeStruct((4, HALF, HD), jnp.bfloat16)],
        in_specs=[SMEM, VMEM] + [ANY] * 2 + [VMEM] * 2,
        out_specs=[VMEM] * 5,
        scratch_shapes=[
            pltpu.VMEM((4, 2, ROWS, HD), jnp.bfloat16),
            pltpu.VMEM((HD, 4 * ROWS), jnp.float32),
            pltpu.VMEM((8, 4 * ROWS), jnp.float32),
            pltpu.SemaphoreType.DMA((2,)),
        ],
        cost_estimate=pl.CostEstimate(
            flops=2_000_000 * 512, bytes_accessed=4 << 20, transcendentals=2_000_000
        ),
        name="attend_late",
        compiler_params=pltpu.CompilerParams(vmem_limit_bytes=67_043_328),
    )(blocks, fq, *pools, acc, row)


def project_kernel(far, ordered, a0, ap, am, a2a, a2b, mine, other, out, at, wt, sems):
    core = lax.axis_index("core")
    _, yh, _, head = places()
    head = 2 * yh if ordered else head
    x = lax.axis_index("x")
    half = lax.axis_index("zhi") ^ far
    copies = Copies(sems)
    for source, step, k0 in ((a0, 0, 0), (ap, 3, 0), (am, 1, 0), (a2a, 2, 0), (a2b, 2, 2)):
        for k in range(source.shape[0]):
            col = ((x + step) % 4) * 512 + (head ^ (k0 + k)) * HD
            copies.start(source.at[k], at.at[:, pl.ds(pl.multiple_of(col, HD), HD)])
    parts = (slice(0, 512), slice(512, COLS))
    loads = []
    for m, part in enumerate(parts):
        for n in range(4):
            target = wt.at[pl.ds(512 * n, 512), part]
            sem = sems.at[copies.used + 4 * m + n]
            one = pltpu.make_async_copy(mine.at[n, :, part], target, sem)
            two = pltpu.make_async_copy(other.at[n, :, part], target, sem)
            pl.when(half == core)(one.start)
            pl.when(half != core)(two.start)
            loads.append(one)
    copies.wait()
    for m, part in enumerate(parts):
        for one in loads[4 * m : 4 * m + 4]:
            one.wait()

        def tile(n, carry):
            rows = pl.ds(pl.multiple_of(n * 128, 128), 128)
            out[rows, part] = jnp.dot(
                at[rows, :], wt[:, part], preferred_element_type=jnp.float32
            ).astype(out.dtype)
            return carry

        lax.fori_loop(0, HALF // 128, tile, 0)


def project(far, ordered, dtype, pieces, weights):
    return pl.pallas_call(
        functools.partial(project_kernel, far, ordered),
        out_shape=jax.ShapeDtypeStruct((HALF, COLS), dtype),
        in_specs=[ANY] * 7,
        out_specs=VMEM,
        scratch_shapes=[
            pltpu.VMEM((HALF, 2048), jnp.bfloat16),
            pltpu.VMEM((2048, COLS), jnp.bfloat16),
            pltpu.SemaphoreType.DMA((24,)),
        ],
        cost_estimate=pl.CostEstimate(
            flops=2 * HALF * 2048 * COLS, bytes_accessed=5 << 20, transcendentals=0
        ),
        name=f"project{ordered}_" + ("far" if far else "near"),
        compiler_params=pltpu.CompilerParams(vmem_limit_bytes=67_043_328),
    )(*pieces, *weights)


def merge(stats, count):
    mean = sum(s[0] for s in stats) / len(stats)
    square = sum(s[1] + count * jnp.square(s[0] - mean) for s in stats)
    return jnp.stack([mean, square])


def shards(
    queries, new_keys, new_values, pool_keys, pool_values, cache_len, cached_table, free_blocks,
    residual_in, out_weight, out_bias, ln_gain, ln_bias,
):
    after = lambda value, *others: lax.optimization_barrier((value, *others))[0]
    group = ("ylo", "core")
    fq, c0, c1, cy = prep(free_blocks, queries, pool_keys, pool_values)

    fq = lax.all_to_all(fq, group, 0, 0)
    cy = move(cy, ("ylo",))
    g0 = jnp.stack([c0, move(c1, ("core",))])
    y0, z0 = move(g0, ("yhi", "ylo")), move(g0, ("zlo",))
    part, keys_out, values_out, f0, f1, fy, early, mid, late = side(
        after(jnp.zeros((1,), jnp.int32), cy), free_blocks, cached_table, cache_len,
        new_keys, new_values, pool_keys, pool_values, out_weight,
    )

    g1 = after(jnp.stack([cy[0], move(cy[1], ("core",))]), y0, z0)
    y1, z1 = move(g1, ("yhi", "ylo")), move(g1, ("zlo",))
    d0 = move(after(y0, g1), ("zlo",))
    fy = move(after(fy, g1), ("ylo",))
    f1 = move(after(f1, g1), ("core",))
    f3 = move(fy[1], ("core",))

    mine = lax.all_to_all(after(part, g1, fq), "x", 0, 0)

    acc, row = attend_early(early, fq, (g0, g1, y0, z0))
    d1 = move(after(z1, acc), ("yhi", "ylo"))
    acc, row = attend_fresh(mid, fq, (f0, f1, fy, f3), (y1, z1), acc, row)
    *mixed0, mixed1 = attend_late(late, fq, (d0, d1), acc, row)

    sums = []
    for ordered, o in enumerate((mixed0, mixed1)):
        if ordered:
            a0 = lax.all_to_all(o, group, 0, 0)
        else:
            a0 = jnp.stack([o[0]] + [move(o[r], RELATION[r]) for r in (1, 2, 3)])
            other = move(after(mine, a0), ("core",))
        ap, am = move(a0, (), 1), move(a0, (), 3)
        pieces = (a0, ap, am, move(ap[:2], (), 1), move(am[2:], (), 3))
        sent = move(project(1, ordered, jnp.bfloat16, pieces, (mine, other)), ("zhi",))
        near = project(0, ordered, jnp.float32, pieces, (mine, other))
        sums.append(near + sent.astype(jnp.float32))
    stream = (
        residual_in.astype(jnp.float32) + jnp.concatenate(sums, axis=0) + out_bias[None, :]
    )
    mean = jnp.sum(stream, axis=1) / COLS
    square = jnp.sum(jnp.square(stream - mean[:, None]), axis=1)
    stats = jnp.stack([mean, square])
    stats = merge([stats] + [move(stats, (), k) for k in (1, 2, 3)], COLS)
    stats = merge([stats, move(stats, ("zhi",))], 4 * COLS)
    mean, variance = stats[0], stats[1] / D
    normed = (
        (stream - mean[:, None]) * lax.rsqrt(variance[:, None] + 1e-05) * ln_gain[None, :]
        + ln_bias[None, :]
    ).astype(jnp.bfloat16)
    return (stream.astype(jnp.bfloat16), normed, keys_out, values_out)


def solution(mesh):
    fine = Mesh(mesh.devices.reshape(tuple(SIZES.values())), tuple(SIZES))
    both = P(SEQ, HEAD)
    head = P(HEAD)
    in_specs = (both,) * 5 + (P(), P(), P()) + (both, P(HEAD, None), head, head, head)
    return jax.shard_map(
        shards, mesh=fine, in_specs=in_specs, out_specs=(both,) * 4, check_vma=False
    )
```
